256 devices in a mesh: row: 32 (over z, x_hi, core), col: 8 (over y, x_lo).
Axes of the slice: x: 4 (x_hi: 2, x_lo: 2; x = x_hi * 2 + x_lo), y: 4, z: 8, core: 2. Of those that a mesh axis runs over, the one named last changes fastest.
Arguments:
- object_field: float32 [2, 2, 4096, 1024], P(None, None, 'row', 'col'), may hold values from -1 to 1
- probe: float32 [4, 2, 128, 128], replicated, may hold values from -3 to 3
- kernel_phase: float32 [128, 128], replicated, may hold values from -3.140625 to 3.140625
- amplitudes: float32 [3, 32, 8, 128, 128], P(None, 'row', 'col'), may hold values from 0.05 to 1
- offsets: int32 [3, 32, 8, 2], P(None, 'row', 'col'), may hold values from 0 to 64
Outputs:
- object_out: float32 [2, 2, 4096, 1024], P(None, None, 'row', 'col')
- probe_out: float32 [4, 2, 128, 128], replicated
The draws below stay inside these ranges and needn't reach their ends.
Inputs may be any that keep to these rules, and one draw needn't show every extreme that they name: offsets[b, r + p, c] place a window of 128 x 128 pixels inside tile (r, c) extended by 32 pixels on each side.
All inputs are finite; a program needn't handle non-finite values.
Results may differ from the reference program's by a relative error of at most 0.0003.
Values sent between devices are 32-bit elements; how exact they have to be, the bound alone decides.
No kernel may reach another device: no remote copies, remote signals or barrier semaphores. Data moves between devices by JAX's collectives and lax.ppermute only.
A program may use at most 128 MiB of HBM per device.

```python
import math
import jax
import jax.numpy as jnp
from jax import lax

TILE = 128
WIN = 128
OVL = 32
MODES = 4
SLICES = 2
BATCHES = 3
NPOS = 1
OBJ_ROWS = 4096
OBJ_COLS = 1024
POS_ROWS = 32
N_ROW = 32
N_COL = 8


def plant(values, stream_key, least, top_value):
    shape = values.shape
    index_at = [jax.random.randint(jax.random.fold_in(stream_key, axis), (), 0, shape[axis]) for axis in range(len(shape))]
    values = values.at[tuple(index_at)].set(least)
    longest = shape.index(max(shape))
    index_at[longest] = (index_at[longest] + 1) % shape[longest]
    return values.at[tuple(index_at)].set(top_value)


def block_levels(own_key, extent, shards, smallest, largest):
    def one(axis_at, parts):
        heights = jax.random.uniform(jax.random.fold_in(jax.random.fold_in(own_key, 6), axis_at), (parts,), jnp.float32, smallest / len(shards), largest / len(shards))
        return jnp.repeat(jnp.exp(heights), extent[axis_at] // parts).reshape((-1,) + (1,) * (len(extent) - axis_at - 1))

    factor_of = one(*shards[0])
    for cut in shards[1:]:
        factor_of = factor_of * one(*cut)
    return factor_of


def scatter_about(rng, extent, deviation, bound, held_as=jnp.bfloat16):
    return jnp.clip(deviation * jax.random.normal(rng, extent, jnp.float32), -bound, bound).astype(held_as)


def setup_inputs(seed: int = 0) -> dict:
    key_of = jax.random.split(jax.random.key(seed), 6)
    return {
        "object_field": jnp.clip(jax.random.uniform(key_of[0], (SLICES, 2, OBJ_ROWS, OBJ_COLS), jnp.float32, -1.0, 1.0) * block_levels(key_of[0], (SLICES, 2, OBJ_ROWS, OBJ_COLS), ((2, 32), (3, 8)), -0.4, 0.0), -1.0, 1.0),
        "probe": scatter_about(key_of[1], (MODES, 2, WIN, WIN), 0.5, 3.0, jnp.float32),
        "kernel_phase": jnp.clip(jax.random.uniform(key_of[2], (WIN, WIN), jnp.float32, -3.140625, 3.140625), -3.140625, 3.140625),
        "amplitudes": jnp.clip(jnp.exp(math.log(1.0) - 2.9957323 * jax.random.uniform(key_of[3], (BATCHES, POS_ROWS, N_COL, WIN, WIN), jnp.float32) ** block_levels(key_of[3], (BATCHES, POS_ROWS, N_COL, WIN, WIN), ((1, 32), (2, 8)), -0.2, 0.2)), 0.05, 1.0),
        "offsets": plant(jax.random.randint(key_of[4], (BATCHES, POS_ROWS, N_COL, 2), 0, 2 * OVL + 1), jax.random.fold_in(key_of[4], 1), 0, 2 * OVL).astype(jnp.int32),
    }


OBJECT_RATE = 0.5
PROBE_RATE = 0.5
FLOOR = 0.1

def spread_wave(field, kernel):
    return jnp.fft.ifft2(jnp.fft.fft2(field, norm='ortho') * kernel, norm='ortho')

def window_gradients(object_window, probe_wave, kernel, measured):
    first_slice = object_window[0, 0] + 1j * object_window[0, 1]
    second_slice = object_window[1, 0] + 1j * object_window[1, 1]
    entrance = probe_wave * first_slice
    spread = spread_wave(entrance, kernel)
    exit_wave = spread * second_slice
    farfield = jnp.fft.fft2(exit_wave, norm='ortho')
    intensity = lax.optimization_barrier(jnp.sum(jnp.real(farfield) ** 2 + jnp.imag(farfield) ** 2, axis=0))
    factor = 1.0 - measured / jnp.sqrt(intensity + FLOOR)
    back_second = jnp.fft.ifft2(farfield * factor, norm='ortho')
    grad_second = lax.optimization_barrier(jnp.sum(jnp.conj(spread) * back_second, axis=0))
    back_first = spread_wave(jnp.conj(second_slice) * back_second, jnp.conj(kernel))
    grad_first = lax.optimization_barrier(jnp.sum(jnp.conj(probe_wave) * back_first, axis=0))
    grad_probe = jnp.conj(first_slice) * back_first
    object_grad = jnp.stack([jnp.stack([jnp.real(grad_first), jnp.imag(grad_first)]), jnp.stack([jnp.real(grad_second), jnp.imag(grad_second)])])
    probe_grad = jnp.stack([jnp.real(grad_probe), jnp.imag(grad_probe)], axis=1)
    return (object_grad, probe_grad)

def reference(object_field, probe, kernel_phase, amplitudes, offsets):
    kernel = jnp.cos(kernel_phase) + 1j * jnp.sin(kernel_phase)
    probe_rate = PROBE_RATE / math.sqrt(N_ROW * N_COL * NPOS)
    windows_total = N_ROW * N_COL * NPOS
    current = object_field
    probe_now = probe
    pending = jnp.zeros_like(probe)
    for batch_index in range(BATCHES):
        padded = jnp.pad(current, ((0, 0), (0, 0), (OVL, OVL), (OVL, OVL)))
        probe_wave = probe_now[:, 0] + 1j * probe_now[:, 1]

        def visit(carry, window_index):
            object_sum, probe_sum = carry
            slot_index = window_index // N_COL
            column_index = window_index % N_COL
            tile_row = slot_index // NPOS
            offset_pair = offsets[batch_index, slot_index, column_index]
            top_row = (tile_row * TILE + offset_pair[0]).astype(jnp.int32)
            left_col = (column_index * TILE + offset_pair[1]).astype(jnp.int32)
            anchor = jnp.zeros((), jnp.int32)
            starts = (anchor, anchor, top_row, left_col)
            window_shape = (SLICES, 2, WIN, WIN)
            object_window = lax.dynamic_slice(padded, starts, window_shape)
            measured = amplitudes[batch_index, slot_index, column_index]
            object_grad, probe_grad = window_gradients(object_window, probe_wave, kernel, measured)
            previous = lax.dynamic_slice(object_sum, starts, window_shape)
            object_sum = lax.dynamic_update_slice(object_sum, previous + object_grad, starts)
            return ((object_sum, probe_sum + probe_grad), None)
        initial = (jnp.zeros_like(padded), jnp.zeros_like(probe))
        (object_sum, probe_sum), unused = lax.scan(visit, initial, jnp.arange(windows_total, dtype=jnp.int32))
        current = current - OBJECT_RATE * object_sum[:, :, OVL:OVL + TILE * N_ROW, OVL:OVL + TILE * N_COL]
        probe_now = probe_now - probe_rate * pending
        pending = probe_sum
    probe_now = probe_now - probe_rate * pending
    return (current, probe_now)
```

```python
import math

import jax
import jax.numpy as jnp
import numpy as np
from jax import lax
from jax.experimental import pallas as pl
from jax.experimental.pallas import tpu as pltpu
from jax.sharding import Mesh, PartitionSpec as P

WIN = 128
OVL = 32
EXT = WIN + 2 * OVL
TALL = EXT + 8
MODES = 4
OBJECT_RATE = 0.5
PROBE_RATE = 0.5
FLOOR = 0.1

AXES = ("z", "xh", "core", "y", "xl")
SIZES = (8, 2, 2, 4, 2)
ROW = ("z", "xh", "core")
COL = ("y", "xl")
CHIPS = ("z", "xh", "y", "xl")
N_ROW = 32
N_COL = 8
N_CHIPS = 128

F32 = jnp.float32
BF16 = jnp.bfloat16


def dft_tables():
    counter = np.arange(WIN, dtype=np.int64)
    phase = (counter[:, None] * counter[None, :] % WIN).astype(np.float64) * (-2.0 * math.pi / WIN)
    cosine = np.cos(phase) / math.sqrt(WIN)
    sine = np.sin(phase) / math.sqrt(WIN)
    forward = np.block([[cosine, sine], [-sine, cosine]])
    out = []
    for table in (forward, forward.T):
        high = table.astype(np.float32).astype(jnp.bfloat16)
        low = (table - high.astype(np.float64)).astype(np.float32).astype(jnp.bfloat16)
        out += [high, low]
    return np.stack(out)


def lanes(shape):
    return lax.broadcasted_iota(jnp.int32, shape, len(shape) - 1)


def split(x):
    high = x.astype(BF16)
    return high, (x - high.astype(F32)).astype(BF16)


def dot(a, b):
    return lax.dot_general(a, b, (((1,), (0,)), ((), ())), preferred_element_type=F32)


def grid_of(blocks):
    return jnp.concatenate([jnp.concatenate(line, axis=1) for line in blocks], axis=0)


def blocks_of(x):
    half = WIN
    return [[x[:half, :half], x[:half, half:]], [x[half:, :half], x[half:, half:]]]


def transposed(blocks):
    return [[blocks[0][0], blocks[1][0]], [blocks[0][1], blocks[1][1]]]


def apply_right(pairs, high, low):
    out = []
    for blocks in pairs:
        xh, xl = split(grid_of(blocks))
        out.append(blocks_of(dot(xh, high) + dot(xh, low) + dot(xl, high)))
    return out


def apply_left(pairs, high, low):
    out = []
    for blocks in pairs:
        xh, xl = split(grid_of(transposed(blocks)))
        out.append(transposed(blocks_of(dot(high, xh) + dot(low, xh) + dot(high, xl))))
    return out


def product(a, b):
    return [a[0] * b[0] - a[1] * b[1], a[0] * b[1] + a[1] * b[0]]


def conj_product(a, b):
    return [a[0] * b[0] + a[1] * b[1], a[0] * b[1] - a[1] * b[0]]


def per_mode(pairs, fn):
    return [[fn(pairs[m // 2][m % 2], m) for m in (2 * k, 2 * k + 1)] for k in range(2)]


def place_window(e_ref, oy, ox, which):
    base = pl.multiple_of(oy // 8 * 8, 8)
    up = (WIN + 8 - oy % 8) % (WIN + 8)
    back = (WIN - ox) % WIN
    parts = []
    for t in range(2):
        rows = e_ref[which, pl.ds(base, WIN + 8), t * WIN : (t + 1) * WIN]
        parts.append(pltpu.roll(pltpu.roll(rows, up, 0)[:WIN], back, 1))
    first, second = parts
    return jnp.where(lanes((WIN, WIN)) < WIN - ox, first, second)


def pack_cols(tile):
    half = EXT // 2
    lane = lanes((half, WIN))
    return jnp.where(lane < 64, tile[:half], pltpu.roll(tile[half:], 64, 1))


def unpack_cols(packed):
    low = lanes(packed.shape) < 64
    return jnp.concatenate(
        [jnp.where(low, packed, 0.0), jnp.where(low, pltpu.roll(packed, 64, 1), 0.0)], axis=0
    )


def pack_rows(first, second):
    lane = lanes((32, WIN))
    rest = jnp.where(lane < 64, second[:32], pltpu.roll(second[32:], 64, 1))
    return jnp.concatenate([first, rest], axis=0)


def unpack_rows(packed):
    rest = packed[64:]
    low = lanes(rest.shape) < 64
    second = jnp.concatenate(
        [jnp.where(low, rest, 0.0), jnp.where(low, pltpu.roll(rest, 64, 1), 0.0)], axis=0
    )
    return packed[:64], second


def halo_kernel(obj, north, south, left, right):
    lane = lanes((48, WIN)) // 32
    for a in range(4):
        column = jnp.concatenate([north[a], obj[a], south[a]], axis=0)
        for ref, base in ((left, 0), (right, 32)):
            out = jnp.zeros((48, WIN), F32)
            for i in range(4):
                part = column[48 * i : 48 * i + 48]
                shift = (32 * i + base) % WIN
                part = pltpu.roll(part, shift, 1) if shift else part
                out = jnp.where(lane == i, part, out)
            ref[a] = out


def build_extended(e_ref, obj, north, south, west, east):
    lane = lanes((EXT, WIN))
    for a in range(4):
        column = jnp.concatenate([north[a], obj[a], south[a]], axis=0)
        column = pltpu.roll(column, 32, 1)
        lefts, rights = [], []
        for i in range(4):
            shift = (WIN - 32 * i) % WIN
            lefts.append(pltpu.roll(west[a], shift, 1) if shift else west[a])
            shift = (32 - 32 * i) % WIN
            rights.append(pltpu.roll(east[a], shift, 1) if shift else east[a])
        e_ref[a, :EXT, :WIN] = jnp.where(lane < 32, jnp.concatenate(lefts, axis=0), column)
        e_ref[a, :EXT, WIN:] = jnp.where(
            lane < 32, column, jnp.where(lane < 64, jnp.concatenate(rights, axis=0), 0.0)
        )


def update_extended(e_ref, info, old, grad, north, south):
    row = lax.broadcasted_iota(jnp.int32, (EXT, WIN), 0)
    lane = lanes((EXT, WIN))
    in_rows = (row >= info[2]) & (row < info[3])
    keep = (in_rows & (lane >= info[4]), in_rows & (lane + WIN < info[5]))
    gap = jnp.zeros((64, WIN), F32)
    for a in range(4):
        n_parts = unpack_rows(north[a])
        s_parts = unpack_rows(south[a])
        for t in range(2):
            cols = slice(t * WIN, (t + 1) * WIN)
            bands = jnp.concatenate([n_parts[t], gap, s_parts[t]], axis=0)
            value = old[a, :EXT, cols] - OBJECT_RATE * (grad[a, :EXT, cols] + bands)
            e_ref[a, :EXT, cols] = jnp.where(keep[t], value, 0.0)


def step_core(info, e_ref, probe, kernel, measured, tables, g_ref, left, right):
    oy, ox = info[0], info[1]
    a_high, a_low, b_high, b_low = (tables[i] for i in range(4))
    o1 = [place_window(e_ref, oy, ox, 0), place_window(e_ref, oy, ox, 1)]
    o2 = [place_window(e_ref, oy, ox, 2), place_window(e_ref, oy, ox, 3)]
    phase = [kernel[0], kernel[1]]
    x = per_mode(probe, lambda p, m: product(p, o1))
    x = apply_left(apply_right(x, a_high, a_low), b_high, b_low)
    x = per_mode(x, lambda v, m: product(phase, v))
    phi = apply_right(apply_left(x, a_high, a_low), b_high, b_low)
    x = per_mode(phi, lambda v, m: product(v, o2))
    x = apply_left(apply_right(x, a_high, a_low), b_high, b_low)
    intensity = sum(x[m // 2][m % 2][c] * x[m // 2][m % 2][c] for m in range(MODES) for c in range(2))
    factor = 1.0 - measured / jnp.sqrt(intensity + FLOOR)
    x = per_mode(x, lambda v, m: [v[0] * factor, v[1] * factor])
    chi2 = apply_right(apply_left(x, a_high, a_low), b_high, b_low)
    terms2 = [conj_product(phi[m // 2][m % 2], chi2[m // 2][m % 2]) for m in range(MODES)]
    x = per_mode(chi2, lambda v, m: conj_product(o2, v))
    x = apply_left(apply_right(x, a_high, a_low), b_high, b_low)
    x = per_mode(x, lambda v, m: conj_product(phase, v))
    chi1 = apply_right(apply_left(x, a_high, a_low), b_high, b_low)
    terms1 = [conj_product(probe[m // 2][m % 2], chi1[m // 2][m % 2]) for m in range(MODES)]
    grads = [sum(t[c] for t in terms1) for c in range(2)] + [sum(t[c] for t in terms2) for c in range(2)]
    lane = lanes((WIN, WIN))
    base = pl.multiple_of(oy // 8 * 8, 8)
    gap = jnp.zeros((8, WIN), F32)
    for a in range(4):
        g_ref[a] = jnp.zeros((TALL, 2 * WIN), F32)
        turned = pltpu.roll(grads[a], ox, 1)
        for t in range(2):
            part = jnp.where(lane >= ox if t == 0 else lane < ox, turned, 0.0)
            part = pltpu.roll(jnp.concatenate([part, gap], axis=0), oy % 8, 0)
            g_ref[a, pl.ds(base, WIN + 8), t * WIN : (t + 1) * WIN] = part
        left[a] = pack_cols(g_ref[a, :EXT, :WIN])
        right[a] = pack_cols(g_ref[a, :EXT, WIN:])
    return per_mode(chi1, lambda v, m: conj_product(o1, v))


def probe_blocks(probe_ref):
    return [[[probe_ref[2 * m], probe_ref[2 * m + 1]] for m in (2 * k, 2 * k + 1)] for k in range(2)]


def write_halves(info, grads, keep, send, add=None):
    first = info[6] == 0
    for i in range(4):
        low = grads[0][i // 2][i % 2]
        high = grads[1][i // 2][i % 2]
        kept = jnp.where(first, low, high)
        sent = jnp.where(first, high, low)
        if add is not None:
            kept = kept + add[0][i]
            sent = sent + add[1][i]
        keep[i] = kept
        send[i] = sent


def first_kernel(info, obj, north, south, west, east, probe, kernel, measured, tables,
                 e_ref, g_ref, left, right, keep, send):
    build_extended(e_ref, obj, north, south, west, east)
    grads = step_core(info, e_ref, probe_blocks(probe), kernel, measured[...], tables, g_ref, left, right)
    write_halves(info, grads, keep, send)


def second_kernel(info, old, grad, north, south, probe, kernel, measured, tables,
                  e_ref, g_ref, left, right, keep, send):
    update_extended(e_ref, info, old, grad, north, south)
    grads = step_core(info, e_ref, probe_blocks(probe), kernel, measured[...], tables, g_ref, left, right)
    write_halves(info, grads, keep, send)


def third_kernel(rate, info, old, grad, north, south, probe, mine, other, keep_add, send_add,
                 kernel, measured, tables,
                 e_ref, g_ref, left, right, keep, send, p_ref):
    update_extended(e_ref, info, old, grad, north, south)
    first = info[6] == 0
    for i in range(4):
        p_ref[i] = probe[i] - rate * jnp.where(first, mine[i], other[i])
        p_ref[4 + i] = probe[4 + i] - rate * jnp.where(first, other[i], mine[i])
    grads = step_core(info, e_ref, probe_blocks(p_ref), kernel, measured[...], tables, g_ref, left, right)
    write_halves(info, grads, keep, send, (keep_add, send_add))


def middle_kernel(g_in, west, east, g_ref, up, down):
    for a in range(4):
        g_ref[a, :EXT, :WIN] = g_in[a, :EXT, :WIN] + unpack_cols(west[a])
        g_ref[a, :EXT, WIN:] = g_in[a, :EXT, WIN:] + unpack_cols(east[a])
        up[a] = pack_rows(g_ref[a, :64, :WIN], g_ref[a, :64, WIN:])
        down[a] = pack_rows(g_ref[a, 128:EXT, :WIN], g_ref[a, 128:EXT, WIN:])


def object_kernel(old, grad, north, south, out):
    lane = lanes((WIN, WIN))
    gap = jnp.zeros((64, WIN), F32)
    for a in range(4):
        n_parts = unpack_rows(north[a])
        s_parts = unpack_rows(south[a])
        parts = []
        for t in range(2):
            cols = slice(t * WIN, (t + 1) * WIN)
            bands = jnp.concatenate([n_parts[t], gap, s_parts[t]], axis=0)
            value = old[a, :EXT, cols] - OBJECT_RATE * (grad[a, :EXT, cols] + bands)
            parts.append(pltpu.roll(value[OVL : OVL + WIN], WIN - OVL, 1))
        out[a] = jnp.where(lane < WIN - OVL, parts[0], parts[1])


def probe_kernel(rate, info, probe, mine, other, out):
    first = info[6] == 0
    for i in range(4):
        out[i] = probe[i] - rate * jnp.where(first, mine[i], other[i])
        out[4 + i] = probe[4 + i] - rate * jnp.where(first, other[i], mine[i])


SMEM = pl.BlockSpec(memory_space=pltpu.SMEM)
VMEM = pl.BlockSpec(memory_space=pltpu.VMEM)


def call(kernel, outs, *args, scalars=0, name=None):
    return pl.pallas_call(
        kernel,
        out_shape=[jax.ShapeDtypeStruct(s, F32) for s in outs],
        in_specs=[SMEM] * scalars + [VMEM] * (len(args) - scalars),
        out_specs=[VMEM] * len(outs),
        name=name,
    )(*args)


EXT_SHAPE = (4, TALL, 2 * WIN)
BAND = (4, EXT // 2, WIN)
HALF = (4, WIN, WIN)


def moved(x, axis, size, distance):
    route = [(i, i + distance) for i in range(size) if 0 <= i + distance < size]
    return lax.ppermute(x, axis, route)


def swap_cores(x):
    return lax.ppermute(x, "core", [(0, 1), (1, 0)])


def summed_half(keep, send):
    total = keep + swap_cores(send)
    parts = lax.all_to_all(total.reshape(N_CHIPS, -1, WIN), CHIPS, 0, 0, tiled=True)
    own = jnp.sum(parts, axis=0)
    whole = lax.all_to_all(
        jnp.broadcast_to(own[None], (N_CHIPS, *own.shape)), CHIPS, 0, 0, tiled=True
    )
    return whole.reshape(HALF)


def exchanged(grad, left, right):
    west = moved(right, COL, N_COL, 1)
    east = moved(left, COL, N_COL, -1)
    grad, up, down = call(middle_kernel, [EXT_SHAPE, BAND, BAND], grad, west, east, name="middle")
    north = moved(down, ROW, N_ROW, 1)
    south = moved(up, ROW, N_ROW, -1)
    return grad, north, south


def per_device(object_field, probe, kernel_phase, amplitudes, offsets):
    rate = PROBE_RATE / math.sqrt(N_ROW * N_COL)
    tables = jnp.asarray(dft_tables())
    kernel = jnp.stack([jnp.cos(kernel_phase), jnp.sin(kernel_phase)])
    row = lax.axis_index(ROW)
    col = lax.axis_index(COL)
    core = lax.axis_index("core")
    edges = jnp.stack([
        jnp.where(row == 0, OVL, 0),
        jnp.where(row == N_ROW - 1, EXT - OVL, EXT),
        jnp.where(col == 0, OVL, 0),
        jnp.where(col == N_COL - 1, EXT - OVL, EXT),
        core,
    ]).astype(jnp.int32)
    infos = [jnp.concatenate([offsets[b, 0, 0], edges]) for b in range(3)]
    measured = amplitudes[:, 0, 0]
    obj = object_field.reshape(4, WIN, WIN)
    probe = probe.reshape(2 * MODES, WIN, WIN)

    north = moved(obj[:, WIN - OVL :], ROW, N_ROW, 1)
    south = moved(obj[:, :OVL], ROW, N_ROW, -1)
    left, right = call(halo_kernel, [(4, 48, WIN)] * 2, obj, north, south, name="halo")
    west = moved(right, COL, N_COL, 1)
    east = moved(left, COL, N_COL, -1)

    step_outs = [EXT_SHAPE, EXT_SHAPE, BAND, BAND, HALF, HALF]
    extended, grad, left, right, keep0, send0 = call(
        first_kernel, step_outs, infos[0], obj, north, south, west, east, probe, kernel,
        measured[0], tables, scalars=1, name="step0",
    )
    grad, north, south = exchanged(grad, left, right)
    mine0 = summed_half(keep0, send0)
    other0 = swap_cores(mine0)
    extended, grad, left, right, keep1, send1 = call(
        second_kernel, step_outs, infos[1], extended, grad, north, south, probe, kernel,
        measured[1], tables, scalars=1, name="step1",
    )
    grad, north, south = exchanged(grad, left, right)
    extended, grad, left, right, keep2, send2, probe = call(
        lambda *refs: third_kernel(rate, *refs), step_outs + [(2 * MODES, WIN, WIN)],
        infos[2], extended, grad, north, south, probe, mine0, other0, keep1, send1, kernel,
        measured[2], tables, scalars=1, name="step2",
    )
    grad, north, south = exchanged(grad, left, right)
    mine = summed_half(keep2, send2)
    other = swap_cores(mine)
    (obj,) = call(object_kernel, [HALF], extended, grad, north, south, name="object")
    (probe,) = call(
        lambda *refs: probe_kernel(rate, *refs), [(2 * MODES, WIN, WIN)],
        infos[2], probe, mine, other, scalars=1, name="probe",
    )
    return obj.reshape(2, 2, WIN, WIN), probe.reshape(MODES, 2, WIN, WIN)


def solution(mesh):
    fine = Mesh(mesh.devices.reshape(SIZES), AXES)
    in_specs = (
        P(None, None, ROW, COL),
        P(),
        P(),
        P(None, ROW, COL, None, None),
        P(None, ROW, COL, None),
    )
    out_specs = (P(None, None, ROW, COL), P())
    return jax.shard_map(
        per_device, mesh=fine, in_specs=in_specs, out_specs=out_specs, check_vma=False
    )
```

```python
import math

import jax
import jax.numpy as jnp
import numpy as np
from jax import lax
from jax.experimental import pallas as pl
from jax.experimental.pallas import tpu as pltpu
from jax.sharding import Mesh, PartitionSpec as P


WIN = 128
OVL = 32
EXT = WIN + 2 * OVL
TALL = EXT + 8
MODES = 4
OBJECT_RATE = 0.5
PROBE_RATE = 0.5
FLOOR = 0.1

AXES = ("z", "xh", "core", "y", "xl")
SIZES = (8, 2, 2, 4, 2)
ROW = ("z", "xh", "core")
COL = ("y", "xl")
CHIPS = ("z", "xh", "y", "xl")
N_ROW = 32
N_COL = 8
N_CHIPS = 128
CORE = 10

F32 = jnp.float32
BF16 = jnp.bfloat16


def dft_tables():
    counter = np.arange(WIN, dtype=np.int64)
    phase = (counter[:, None] * counter[None, :] % WIN).astype(np.float64) * (-2.0 * math.pi / WIN)
    cosine = np.cos(phase) / math.sqrt(WIN)
    sine = np.sin(phase) / math.sqrt(WIN)
    forward = np.block([[cosine, sine], [-sine, cosine]])
    out = []
    for table in (forward, forward.T):
        high = table.astype(np.float32).astype(jnp.bfloat16)
        low = (table - high.astype(np.float64)).astype(np.float32).astype(jnp.bfloat16)
        out += [high, low]
    return np.stack(out)


def lanes(shape):
    return lax.broadcasted_iota(jnp.int32, shape, len(shape) - 1)


def split(x):
    high = x.astype(BF16)
    return high, (x - high.astype(F32)).astype(BF16)


def dot(a, b):
    return lax.dot_general(a, b, (((1,), (0,)), ((), ())), preferred_element_type=F32)


def grid_of(blocks):
    return jnp.concatenate([jnp.concatenate(line, axis=1) for line in blocks], axis=0)


def blocks_of(x):
    half = WIN
    return [[x[:half, :half], x[:half, half:]], [x[half:, :half], x[half:, half:]]]


def transposed(blocks):
    return [[blocks[0][0], blocks[1][0]], [blocks[0][1], blocks[1][1]]]


def apply_right(pairs, high, low):
    out = []
    for blocks in pairs:
        xh, xl = split(grid_of(blocks))
        out.append(blocks_of(dot(xh, high) + dot(xh, low) + dot(xl, high)))
    return out


def apply_left(pairs, high, low):
    out = []
    for blocks in pairs:
        xh, xl = split(grid_of(transposed(blocks)))
        out.append(transposed(blocks_of(dot(high, xh) + dot(low, xh) + dot(high, xl))))
    return out


def product(a, b):
    return [a[0] * b[0] - a[1] * b[1], a[0] * b[1] + a[1] * b[0]]


def conj_product(a, b):
    return [a[0] * b[0] + a[1] * b[1], a[0] * b[1] - a[1] * b[0]]


def per_mode(pairs, fn):
    return [[fn(pairs[m // 2][m % 2], m) for m in (2 * k, 2 * k + 1)] for k in range(2)]


def place_window(e_ref, oy, ox, which):
    base = pl.multiple_of(oy // 8 * 8, 8)
    up = (WIN + 8 - oy % 8) % (WIN + 8)
    back = (WIN - ox) % WIN
    parts = []
    for t in range(2):
        rows = e_ref[which, pl.ds(base, WIN + 8), t * WIN : (t + 1) * WIN]
        parts.append(pltpu.roll(pltpu.roll(rows, up, 0)[:WIN], back, 1))
    first, second = parts
    return jnp.where(lanes((WIN, WIN)) < WIN - ox, first, second)


def pack_cols(tile):
    half = EXT // 2
    lane = lanes((half, WIN))
    return jnp.where(lane < 64, tile[:half], pltpu.roll(tile[half:], 64, 1))


def unpack_cols(packed):
    low = lanes(packed.shape) < 64
    return jnp.concatenate(
        [jnp.where(low, packed, 0.0), jnp.where(low, pltpu.roll(packed, 64, 1), 0.0)], axis=0
    )


def pack_rows(first, second):
    lane = lanes((32, WIN))
    rest = jnp.where(lane < 64, second[:32], pltpu.roll(second[32:], 64, 1))
    return jnp.concatenate([first, rest], axis=0)


def unpack_rows(packed):
    rest = packed[64:]
    low = lanes(rest.shape) < 64
    second = jnp.concatenate(
        [jnp.where(low, rest, 0.0), jnp.where(low, pltpu.roll(rest, 64, 1), 0.0)], axis=0
    )
    return packed[:64], second


def halo_kernel(obj, north, south, left, right):
    lane = lanes((48, WIN)) // 32
    for a in range(4):
        column = jnp.concatenate([north[a], obj[a], south[a]], axis=0)
        for ref, base in ((left, 0), (right, 32)):
            out = jnp.zeros((48, WIN), F32)
            for i in range(4):
                part = column[48 * i : 48 * i + 48]
                shift = (32 * i + base) % WIN
                part = pltpu.roll(part, shift, 1) if shift else part
                out = jnp.where(lane == i, part, out)
            ref[a] = out


def build_extended(e_ref, obj, north, south, west, east):
    lane = lanes((EXT, WIN))
    for a in range(4):
        column = jnp.concatenate([north[a], obj[a], south[a]], axis=0)
        column = pltpu.roll(column, 32, 1)
        lefts, rights = [], []
        for i in range(4):
            shift = (WIN - 32 * i) % WIN
            lefts.append(pltpu.roll(west[a], shift, 1) if shift else west[a])
            shift = (32 - 32 * i) % WIN
            rights.append(pltpu.roll(east[a], shift, 1) if shift else east[a])
        e_ref[a, :EXT, :WIN] = jnp.where(lane < 32, jnp.concatenate(lefts, axis=0), column)
        e_ref[a, :EXT, WIN:] = jnp.where(
            lane < 32, column, jnp.where(lane < 64, jnp.concatenate(rights, axis=0), 0.0)
        )


def update_extended(e_ref, info, old, grad, north, south):
    row = lax.broadcasted_iota(jnp.int32, (EXT, WIN), 0)
    lane = lanes((EXT, WIN))
    in_rows = (row >= info[6]) & (row < info[7])
    keep = (in_rows & (lane >= info[8]), in_rows & (lane + WIN < info[9]))
    gap = jnp.zeros((64, WIN), F32)
    for a in range(4):
        n_parts = unpack_rows(north[a])
        s_parts = unpack_rows(south[a])
        for t in range(2):
            cols = slice(t * WIN, (t + 1) * WIN)
            bands = jnp.concatenate([n_parts[t], gap, s_parts[t]], axis=0)
            value = old[a, :EXT, cols] - OBJECT_RATE * (grad[a, :EXT, cols] + bands)
            e_ref[a, :EXT, cols] = jnp.where(keep[t], value, 0.0)


def step_core(info, b, e_ref, probe, kernel, measured, tables, g_ref, left, right):
    oy, ox = info[2 * b], info[2 * b + 1]
    a_high, a_low, b_high, b_low = (tables[i] for i in range(4))
    o1 = [place_window(e_ref, oy, ox, 0), place_window(e_ref, oy, ox, 1)]
    o2 = [place_window(e_ref, oy, ox, 2), place_window(e_ref, oy, ox, 3)]
    phase = [kernel[0][...], kernel[1][...]]
    x = per_mode(probe, lambda p, m: product(p, o1))
    x = apply_left(apply_right(x, a_high, a_low), b_high, b_low)
    x = per_mode(x, lambda v, m: product(phase, v))
    phi = apply_right(apply_left(x, a_high, a_low), b_high, b_low)
    x = per_mode(phi, lambda v, m: product(v, o2))
    x = apply_left(apply_right(x, a_high, a_low), b_high, b_low)
    intensity = sum(x[m // 2][m % 2][c] * x[m // 2][m % 2][c] for m in range(MODES) for c in range(2))
    factor = 1.0 - measured[b] / jnp.sqrt(intensity + FLOOR)
    x = per_mode(x, lambda v, m: [v[0] * factor, v[1] * factor])
    chi2 = apply_right(apply_left(x, a_high, a_low), b_high, b_low)
    terms2 = [conj_product(phi[m // 2][m % 2], chi2[m // 2][m % 2]) for m in range(MODES)]
    x = per_mode(chi2, lambda v, m: conj_product(o2, v))
    x = apply_left(apply_right(x, a_high, a_low), b_high, b_low)
    x = per_mode(x, lambda v, m: conj_product(phase, v))
    chi1 = apply_right(apply_left(x, a_high, a_low), b_high, b_low)
    terms1 = [conj_product(probe[m // 2][m % 2], chi1[m // 2][m % 2]) for m in range(MODES)]
    grads = [sum(t[c] for t in terms1) for c in range(2)] + [sum(t[c] for t in terms2) for c in range(2)]
    lane = lanes((WIN, WIN))
    base = pl.multiple_of(oy // 8 * 8, 8)
    gap = jnp.zeros((8, WIN), F32)
    for a in range(4):
        g_ref[a] = jnp.zeros((TALL, 2 * WIN), F32)
        turned = pltpu.roll(grads[a], ox, 1)
        for t in range(2):
            part = jnp.where(lane >= ox if t == 0 else lane < ox, turned, 0.0)
            part = pltpu.roll(jnp.concatenate([part, gap], axis=0), oy % 8, 0)
            g_ref[a, pl.ds(base, WIN + 8), t * WIN : (t + 1) * WIN] = part
        left[a] = pack_cols(g_ref[a, :EXT, :WIN])
        right[a] = pack_cols(g_ref[a, :EXT, WIN:])
    return per_mode(chi1, lambda v, m: conj_product(o1, v))


def probe_blocks(probe_ref):
    return [[[probe_ref[2 * m], probe_ref[2 * m + 1]] for m in (2 * k, 2 * k + 1)] for k in range(2)]


def write_halves(info, grads, keep, send, add=None):
    first = info[CORE] == 0
    for i in range(4):
        low = grads[0][i // 2][i % 2]
        high = grads[1][i // 2][i % 2]
        kept = jnp.where(first, low, high)
        sent = jnp.where(first, high, low)
        if add is not None:
            kept = kept + add[0][i]
            sent = sent + add[1][i]
        keep[i] = kept
        send[i] = sent


def first_kernel(info, obj, north, south, west, east, probe, kcos, ksin, measured, tables,
                 e_ref, g_ref, left, right, keep, send):
    build_extended(e_ref, obj, north, south, west, east)
    grads = step_core(info, 0, e_ref, probe_blocks(probe), (kcos, ksin), measured, tables, g_ref, left, right)
    write_halves(info, grads, keep, send)


def second_kernel(info, old, grad, north, south, probe, kcos, ksin, measured, tables,
                  e_ref, g_ref, left, right, keep, send):
    update_extended(e_ref, info, old, grad, north, south)
    grads = step_core(info, 1, e_ref, probe_blocks(probe), (kcos, ksin), measured, tables, g_ref, left, right)
    write_halves(info, grads, keep, send)


def third_kernel(rate, info, old, grad, north, south, probe, mine, other, keep_add, send_add,
                 kcos, ksin, measured, tables,
                 e_ref, g_ref, left, right, keep, send, p_ref):
    update_extended(e_ref, info, old, grad, north, south)
    update_probe(rate, info, probe, mine, other, p_ref)
    grads = step_core(info, 2, e_ref, probe_blocks(p_ref), (kcos, ksin), measured, tables, g_ref, left, right)
    write_halves(info, grads, keep, send, (keep_add, send_add))


def update_probe(rate, info, probe, mine, other, out):
    first = info[CORE] == 0
    for i in range(4):
        out[i] = probe[i] - rate * jnp.where(first, mine[i], other[i])
        out[4 + i] = probe[4 + i] - rate * jnp.where(first, other[i], mine[i])


def middle_kernel(g_in, west, east, g_ref, up, down):
    for a in range(4):
        g_ref[a, :EXT, :WIN] = g_in[a, :EXT, :WIN] + unpack_cols(west[a])
        g_ref[a, :EXT, WIN:] = g_in[a, :EXT, WIN:] + unpack_cols(east[a])
        up[a] = pack_rows(g_ref[a, :64, :WIN], g_ref[a, :64, WIN:])
        down[a] = pack_rows(g_ref[a, 128:EXT, :WIN], g_ref[a, 128:EXT, WIN:])


def object_kernel(old, grad, north, south, out):
    lane = lanes((WIN, WIN))
    gap = jnp.zeros((64, WIN), F32)
    for a in range(4):
        n_parts = unpack_rows(north[a])
        s_parts = unpack_rows(south[a])
        parts = []
        for t in range(2):
            cols = slice(t * WIN, (t + 1) * WIN)
            bands = jnp.concatenate([n_parts[t], gap, s_parts[t]], axis=0)
            value = old[a, :EXT, cols] - OBJECT_RATE * (grad[a, :EXT, cols] + bands)
            parts.append(pltpu.roll(value[OVL : OVL + WIN], WIN - OVL, 1))
        out[a] = jnp.where(lane < WIN - OVL, parts[0], parts[1])


SMEM = pl.BlockSpec(memory_space=pltpu.SMEM)
VMEM = pl.BlockSpec(memory_space=pltpu.VMEM)


def call(kernel, outs, *args, scalars=0, on_chip=True):
    args = list(args[:scalars]) + [
        pltpu.with_memory_space_constraint(x, pltpu.VMEM) for x in args[scalars:]
    ]
    return pl.pallas_call(
        kernel,
        out_shape=[pltpu.VMEM(s, F32) if on_chip else jax.ShapeDtypeStruct(s, F32) for s in outs],
        in_specs=[SMEM] * scalars + [VMEM] * (len(args) - scalars),
        out_specs=[VMEM] * len(outs),
        compiler_params=pltpu.CompilerParams(vmem_limit_bytes=32 << 20),
    )(*args)


EXT_SHAPE = (4, TALL, 2 * WIN)
BAND = (4, EXT // 2, WIN)
HALF = (4, WIN, WIN)


def moved(x, axis, size, distance):
    route = [(i, i + distance) for i in range(size) if 0 <= i + distance < size]
    return lax.ppermute(x, axis, route)


def swap_cores(x):
    return lax.ppermute(x, "core", [(0, 1), (1, 0)])


def chip_exchange(x):
    return lax.all_to_all(x, CHIPS, 0, 0, tiled=True)


def summed_half(keep, send):
    total = keep + swap_cores(send)
    parts = chip_exchange(total.reshape(N_CHIPS, -1, WIN))
    own = jnp.sum(parts, axis=0)
    spread = jnp.broadcast_to(own[None], (N_CHIPS, *own.shape))
    return chip_exchange(spread).reshape(HALF)


def exchanged(grad, left, right):
    west = moved(right, COL, N_COL, 1)
    east = moved(left, COL, N_COL, -1)
    grad, up, down = call(middle_kernel, [EXT_SHAPE, BAND, BAND], grad, west, east)
    north = moved(down, ROW, N_ROW, 1)
    south = moved(up, ROW, N_ROW, -1)
    return grad, north, south


def steps(object_field, probe, kernel_phase, amplitudes, offsets):
    rate = PROBE_RATE / math.sqrt(N_ROW * N_COL)
    tables = jnp.asarray(dft_tables())
    kcos, ksin = jnp.cos(kernel_phase), jnp.sin(kernel_phase)
    row = lax.axis_index(ROW)
    col = lax.axis_index(COL)
    core = lax.axis_index("core")
    edges = jnp.stack([
        jnp.where(row == 0, OVL, 0),
        jnp.where(row == N_ROW - 1, EXT - OVL, EXT),
        jnp.where(col == 0, OVL, 0),
        jnp.where(col == N_COL - 1, EXT - OVL, EXT),
        core,
    ]).astype(jnp.int32)
    info = jnp.concatenate([offsets.reshape(-1), edges])
    measured = amplitudes[:, 0, 0]
    obj = object_field.reshape(4, WIN, WIN)
    probe = probe.reshape(2 * MODES, WIN, WIN)

    north = moved(obj[:, WIN - OVL :], ROW, N_ROW, 1)
    south = moved(obj[:, :OVL], ROW, N_ROW, -1)
    left, right = call(halo_kernel, [(4, 48, WIN)] * 2, obj, north, south)
    west = moved(right, COL, N_COL, 1)
    east = moved(left, COL, N_COL, -1)

    step_outs = [EXT_SHAPE, EXT_SHAPE, BAND, BAND, HALF, HALF]
    extended, grad, left, right, keep0, send0 = call(
        first_kernel, step_outs, info, obj, north, south, west, east, probe, kcos, ksin,
        measured, tables, scalars=1,
    )
    grad, north, south = exchanged(grad, left, right)
    mine0 = summed_half(keep0, send0)
    other0 = swap_cores(mine0)
    extended, grad, left, right, keep1, send1 = call(
        second_kernel, step_outs, info, extended, grad, north, south, probe, kcos, ksin,
        measured, tables, scalars=1,
    )
    grad, north, south = exchanged(grad, left, right)
    extended, grad, left, right, keep2, send2, probe = call(
        lambda *refs: third_kernel(rate, *refs), step_outs + [(2 * MODES, WIN, WIN)],
        info, extended, grad, north, south, probe, mine0, other0, keep1, send1, kcos, ksin,
        measured, tables, scalars=1,
    )
    grad, north, south = exchanged(grad, left, right)
    mine = summed_half(keep2, send2)
    other = swap_cores(mine)
    (obj,) = call(object_kernel, [HALF], extended, grad, north, south, on_chip=False)
    (probe,) = call(
        lambda *refs: update_probe(rate, *refs), [(2 * MODES, WIN, WIN)],
        info, probe, mine, other, scalars=1, on_chip=False,
    )
    return obj.reshape(2, 2, WIN, WIN), probe.reshape(MODES, 2, WIN, WIN)


def solution(mesh):
    fine = Mesh(mesh.devices.reshape(SIZES), AXES)
    in_specs = (
        P(None, None, ROW, COL),
        P(),
        P(),
        P(None, ROW, COL, None, None),
        P(None, ROW, COL, None),
    )
    out_specs = (P(None, None, ROW, COL), P())
    return jax.shard_map(steps, mesh=fine, in_specs=in_specs, out_specs=out_specs, check_vma=False)
```

```python
import math

import jax
import jax.numpy as jnp
import numpy as np
from jax import lax
from jax.experimental import pallas as pl
from jax.experimental.pallas import tpu as pltpu
from jax.sharding import Mesh, PartitionSpec as P


WIN = 128
OVL = 32
EXT = WIN + 2 * OVL
TALL = EXT + 8
MODES = 4
OBJECT_RATE = 0.5
PROBE_RATE = 0.5
FLOOR = 0.1

AXES = ("z", "xh", "core", "y", "xl")
SIZES = (8, 2, 2, 4, 2)
ROW = ("z", "xh", "core")
COL = ("y", "xl")
CHIPS = ("z", "xh", "y", "xl")
N_ROW = 32
N_COL = 8
N_CHIPS = 128
CORE = 10
XLOW = 11

F32 = jnp.float32
BF16 = jnp.bfloat16


def dft_tables():
    counter = np.arange(WIN, dtype=np.int64)
    phase = (counter[:, None] * counter[None, :] % WIN).astype(np.float64) * (-2.0 * math.pi / WIN)
    out = []
    for table in (np.cos(phase) / math.sqrt(WIN), np.sin(phase) / math.sqrt(WIN)):
        high = table.astype(np.float32).astype(jnp.bfloat16)
        low = (table - high.astype(np.float64)).astype(np.float32).astype(jnp.bfloat16)
        out += [high, low]
    return np.stack(out)


def full_tables(refs):
    out = []
    for part in range(2):
        cosine, sine = refs[part], refs[2 + part]
        out.append(grid_of([[cosine, sine], [-sine, cosine]]))
        out.append(grid_of([[cosine, -sine], [sine, cosine]]))
    return out


def lanes(shape):
    return lax.broadcasted_iota(jnp.int32, shape, len(shape) - 1)


def split(x):
    high = x.astype(BF16)
    return high, (x - high.astype(F32)).astype(BF16)


def dot(a, b):
    return lax.dot_general(a, b, (((1,), (0,)), ((), ())), preferred_element_type=F32)


def grid_of(blocks):
    return jnp.concatenate([jnp.concatenate(line, axis=1) for line in blocks], axis=0)


def blocks_of(x):
    half = WIN
    return [[x[:half, :half], x[:half, half:]], [x[half:, :half], x[half:, half:]]]


def transposed(blocks):
    return [[blocks[0][0], blocks[1][0]], [blocks[0][1], blocks[1][1]]]


def apply_right(pairs, high, low):
    out = []
    for blocks in pairs:
        xh, xl = split(grid_of(blocks))
        out.append(blocks_of(dot(xh, high) + dot(xh, low) + dot(xl, high)))
    return out


def apply_left(pairs, high, low):
    out = []
    for blocks in pairs:
        xh, xl = split(grid_of(transposed(blocks)))
        out.append(transposed(blocks_of(dot(high, xh) + dot(low, xh) + dot(high, xl))))
    return out


def product(a, b):
    return [a[0] * b[0] - a[1] * b[1], a[0] * b[1] + a[1] * b[0]]


def conj_product(a, b):
    return [a[0] * b[0] + a[1] * b[1], a[0] * b[1] - a[1] * b[0]]


def per_mode(pairs, fn):
    return [[fn(pairs[m // 2][m % 2], m) for m in (2 * k, 2 * k + 1)] for k in range(2)]


def place_window(e_ref, oy, ox, which):
    base = pl.multiple_of(oy // 8 * 8, 8)
    up = (WIN + 8 - oy % 8) % (WIN + 8)
    back = (WIN - ox) % WIN
    parts = []
    for t in range(2):
        rows = e_ref[which, pl.ds(base, WIN + 8), t * WIN : (t + 1) * WIN]
        parts.append(pltpu.roll(pltpu.roll(rows, up, 0)[:WIN], back, 1))
    first, second = parts
    return jnp.where(lanes((WIN, WIN)) < WIN - ox, first, second)


def pack_cols(tile):
    half = EXT // 2
    lane = lanes((half, WIN))
    return jnp.where(lane < 64, tile[:half], pltpu.roll(tile[half:], 64, 1))


def unpack_cols(packed):
    low = lanes(packed.shape) < 64
    return jnp.concatenate(
        [jnp.where(low, packed, 0.0), jnp.where(low, pltpu.roll(packed, 64, 1), 0.0)], axis=0
    )


def pack_rows(first, second):
    lane = lanes((32, WIN))
    rest = jnp.where(lane < 64, second[:32], pltpu.roll(second[32:], 64, 1))
    return jnp.concatenate([first, rest], axis=0)


def unpack_rows(packed):
    rest = packed[64:]
    low = lanes(rest.shape) < 64
    second = jnp.concatenate(
        [jnp.where(low, rest, 0.0), jnp.where(low, pltpu.roll(rest, 64, 1), 0.0)], axis=0
    )
    return packed[:64], second


def by_parity(odd, pair, near, far, a):
    first, last = pair
    near[a] = jnp.where(odd, first, last)
    far[a] = jnp.where(odd, last, first)


def sides(odd, near, far, a):
    return jnp.where(odd, near[a], far[a]), jnp.where(odd, far[a], near[a])


def cut_kernel(info, obj, near, far):
    for a in range(4):
        by_parity(info[CORE - 6] == 1, (obj[a, :OVL], obj[a, WIN - OVL :]), near, far, a)


def halo_kernel(info, obj, row_near, row_far, near, far):
    lane = lanes((48, WIN)) // 32
    for a in range(4):
        north, south = sides(info[CORE] == 1, row_near, row_far, a)
        column = jnp.concatenate([north, obj[a], south], axis=0)
        strips = []
        for base in (0, 32):
            out = jnp.zeros((48, WIN), F32)
            for i in range(4):
                part = column[48 * i : 48 * i + 48]
                shift = (32 * i + base) % WIN
                part = pltpu.roll(part, shift, 1) if shift else part
                out = jnp.where(lane == i, part, out)
            strips.append(out)
        by_parity(info[XLOW] == 1, strips, near, far, a)


def build_extended(e_ref, info, obj, row_near, row_far, col_near, col_far):
    lane = lanes((EXT, WIN))
    for a in range(4):
        north, south = sides(info[CORE] == 1, row_near, row_far, a)
        west, east = sides(info[XLOW] == 1, col_near, col_far, a)
        column = jnp.concatenate([north, obj[a], south], axis=0)
        column = pltpu.roll(column, 32, 1)
        lefts, rights = [], []
        for i in range(4):
            shift = (WIN - 32 * i) % WIN
            lefts.append(pltpu.roll(west, shift, 1) if shift else west)
            shift = (32 - 32 * i) % WIN
            rights.append(pltpu.roll(east, shift, 1) if shift else east)
        e_ref[a, :EXT, :WIN] = jnp.where(lane < 32, jnp.concatenate(lefts, axis=0), column)
        e_ref[a, :EXT, WIN:] = jnp.where(
            lane < 32, column, jnp.where(lane < 64, jnp.concatenate(rights, axis=0), 0.0)
        )


def place_gradient(info, b, grads, g_ref):
    oy, ox = info[2 * b], info[2 * b + 1]
    lane = lanes((WIN, WIN))
    base = pl.multiple_of(oy // 8 * 8, 8)
    gap = jnp.zeros((8, WIN), F32)
    for a in range(4):
        g_ref[a] = jnp.zeros((TALL, 2 * WIN), F32)
        turned = pltpu.roll(grads[a], ox, 1)
        for t in range(2):
            part = jnp.where(lane >= ox if t == 0 else lane < ox, turned, 0.0)
            part = pltpu.roll(jnp.concatenate([part, gap], axis=0), oy % 8, 0)
            g_ref[a, pl.ds(base, WIN + 8), t * WIN : (t + 1) * WIN] = part


def row_bands(info, rn, rf, a):
    north, south = (unpack_rows(x) for x in sides(info[CORE] == 1, rn, rf, a))
    gap = jnp.zeros((64, WIN), F32)
    return [jnp.concatenate([north[t], gap, south[t]], axis=0) for t in range(2)]


def total_gradient(info, g_ref, rows, cols, a):
    west_east = sides(info[XLOW] == 1, *cols, a)
    bands = row_bands(info, *rows, a)
    return [
        g_ref[a, :EXT, t * WIN : (t + 1) * WIN] + unpack_cols(west_east[t]) + bands[t]
        for t in range(2)
    ]


def pack_extended(e_ref, out):
    for a in range(4):
        out[a, :EXT] = e_ref[a, :EXT, :WIN]
        out[a, EXT:] = pack_cols(e_ref[a, :EXT, WIN:])


def own_part(parts):
    lane = lanes((WIN, WIN))
    turned = [pltpu.roll(x[OVL : OVL + WIN], WIN - OVL, 1) for x in parts]
    return jnp.where(lane < WIN - OVL, turned[0], turned[1])


def update_extended(e_ref, g_ref, info, b, old, grads, rows, cols):
    place_gradient(info, b - 1, grads, g_ref)
    row = lax.broadcasted_iota(jnp.int32, (EXT, WIN), 0)
    lane = lanes((EXT, WIN))
    in_rows = (row >= info[6]) & (row < info[7])
    keep = (in_rows & (lane >= info[8]), in_rows & (lane + WIN < info[9]))
    for a in range(4):
        grad = total_gradient(info, g_ref, rows, cols, a)
        before = (old[a, :EXT], unpack_cols(old[a, EXT:]))
        for t in range(2):
            value = before[t] - OBJECT_RATE * grad[t]
            e_ref[a, :EXT, t * WIN : (t + 1) * WIN] = jnp.where(keep[t], value, 0.0)


def step_core(info, b, e_ref, probe, loads, kernel, measured, tables, g_ref, w_ref, near, far):
    oy, ox = info[2 * b], info[2 * b + 1]
    o1 = [place_window(e_ref, oy, ox, 0), place_window(e_ref, oy, ox, 1)]
    o2 = [place_window(e_ref, oy, ox, 2), place_window(e_ref, oy, ox, 3)]
    loads[1].wait()
    a_high, b_high, a_low, b_low = full_tables(tables)
    x = per_mode(probe, lambda p, m: product(p, o1))
    for load in loads[2:]:
        load.wait()
    phase = [kernel[0], kernel[1]]
    x = apply_left(apply_right(x, a_high, a_low), b_high, b_low)
    x = per_mode(x, lambda v, m: product(phase, v))
    phi = apply_right(apply_left(x, a_high, a_low), b_high, b_low)
    x = per_mode(phi, lambda v, m: product(v, o2))
    x = apply_left(apply_right(x, a_high, a_low), b_high, b_low)
    intensity = sum(x[m // 2][m % 2][c] * x[m // 2][m % 2][c] for m in range(MODES) for c in range(2))
    factor = 1.0 - measured[...] / jnp.sqrt(intensity + FLOOR)
    x = per_mode(x, lambda v, m: [v[0] * factor, v[1] * factor])
    chi2 = apply_right(apply_left(x, a_high, a_low), b_high, b_low)
    terms2 = [conj_product(phi[m // 2][m % 2], chi2[m // 2][m % 2]) for m in range(MODES)]
    x = per_mode(chi2, lambda v, m: conj_product(o2, v))
    x = apply_left(apply_right(x, a_high, a_low), b_high, b_low)
    x = per_mode(x, lambda v, m: conj_product(phase, v))
    chi1 = apply_right(apply_left(x, a_high, a_low), b_high, b_low)
    terms1 = [conj_product(probe[m // 2][m % 2], chi1[m // 2][m % 2]) for m in range(MODES)]
    grads = [sum(t[c] for t in terms1) for c in range(2)] + [sum(t[c] for t in terms2) for c in range(2)]
    for a in range(4):
        w_ref[a] = grads[a]
    place_gradient(info, b, grads, g_ref)
    for a in range(4):
        up = pack_rows(g_ref[a, :64, :WIN], g_ref[a, :64, WIN:])
        down = pack_rows(g_ref[a, 128:EXT, :WIN], g_ref[a, 128:EXT, WIN:])
        by_parity(info[CORE] == 1, (up, down), near, far, a)
    return per_mode(chi1, lambda v, m: conj_product(o1, v))


def probe_blocks(probe_ref):
    return [[[probe_ref[2 * m], probe_ref[2 * m + 1]] for m in (2 * k, 2 * k + 1)] for k in range(2)]


def write_halves(info, grads, keep, send):
    first = info[CORE] == 0
    for i in range(4):
        low = grads[0][i // 2][i % 2]
        high = grads[1][i // 2][i % 2]
        keep[i] = jnp.where(first, low, high)
        send[i] = jnp.where(first, high, low)


def loads_of(b, probe, tables, kcos, ksin, measured, p_s, t_s, k_s, m_s, sem):
    pairs = (
        (probe, p_s), (tables, t_s), (kcos, k_s.at[0]), (ksin, k_s.at[1]), (measured.at[b], m_s)
    )
    copies = [pltpu.make_async_copy(x, y, sem.at[i]) for i, (x, y) in enumerate(pairs)]
    for copy in copies:
        copy.start()
    return copies


def first_kernel(info, obj, row_near, row_far, col_near, col_far, probe, tables, kcos, ksin, measured,
                 e_out, w_ref, near, far, keep, send, e_s, g_s, p_s, t_s, k_s, m_s, sem):
    loads = loads_of(0, probe, tables, kcos, ksin, measured, p_s, t_s, k_s, m_s, sem)
    build_extended(e_s, info, obj, row_near, row_far, col_near, col_far)
    pack_extended(e_s, e_out)
    loads[0].wait()
    grads = step_core(info, 0, e_s, probe_blocks(p_s), loads, k_s, m_s, t_s, g_s, w_ref, near, far)
    write_halves(info, grads, keep, send)


def second_kernel(info, old, grad, rn, rf, cn, cf, probe, tables, kcos, ksin, measured,
                  e_out, w_ref, near, far, held, e_s, g_s, p_s, t_s, k_s, m_s, h_s, sem):
    loads = loads_of(1, probe, tables, kcos, ksin, measured, p_s, t_s, k_s, m_s, sem)
    update_extended(e_s, g_s, info, 1, old, grad, (rn, rf), (cn, cf))
    pack_extended(e_s, e_out)
    loads[0].wait()
    grads = step_core(info, 1, e_s, probe_blocks(p_s), loads, k_s, m_s, t_s, g_s, w_ref, near, far)
    for m in range(MODES):
        h_s[2 * m] = grads[m // 2][m % 2][0]
        h_s[2 * m + 1] = grads[m // 2][m % 2][1]
    store = pltpu.make_async_copy(h_s, held, sem.at[5])
    store.start()
    store.wait()


def third_kernel(rate, info, old, grad, rn, rf, cn, cf, mine, other,
                 probe, tables, kcos, ksin, measured, held,
                 own, w_ref, near, far, keep, send, p_out, e_s, g_s, p_s, t_s, k_s, m_s, h_s, sem):
    loads = loads_of(2, probe, tables, kcos, ksin, measured, p_s, t_s, k_s, m_s, sem)
    load_held = pltpu.make_async_copy(held, h_s, sem.at[5])
    load_held.start()
    update_extended(e_s, g_s, info, 2, old, grad, (rn, rf), (cn, cf))
    for a in range(4):
        own[a] = own_part((e_s[a, :, :WIN], e_s[a, :, WIN:]))
    loads[0].wait()
    update_probe(rate, info, p_s, mine, other, p_out)
    grads = step_core(info, 2, e_s, probe_blocks(p_out), loads, k_s, m_s, t_s, g_s, w_ref, near, far)
    load_held.wait()
    grads = per_mode(grads, lambda v, m: [v[c] + h_s[2 * m + c] for c in range(2)])
    write_halves(info, grads, keep, send)


def update_probe(rate, info, probe, mine, other, out):
    first = info[CORE] == 0
    for i in range(4):
        out[i] = probe[i] - rate * jnp.where(first, mine[i], other[i])
        out[4 + i] = probe[4 + i] - rate * jnp.where(first, other[i], mine[i])


def middle_kernel(b, info, grad, rn, rf, near, far, g_s):
    place_gradient(info, b, grad, g_s)
    for a in range(4):
        bands = row_bands(info, rn, rf, a)
        strips = [pack_cols(g_s[a, :EXT, t * WIN : (t + 1) * WIN] + bands[t]) for t in range(2)]
        by_parity(info[XLOW] == 1, strips, near, far, a)


def object_kernel(info, own, grad, rn, rf, cn, cf, out, g_s):
    place_gradient(info, 2, grad, g_s)
    for a in range(4):
        total = total_gradient(info, g_s, (rn, rf), (cn, cf), a)
        out[a] = own[a] - OBJECT_RATE * own_part(total)


SMEM = pl.BlockSpec(memory_space=pltpu.SMEM)
VMEM = pl.BlockSpec(memory_space=pltpu.VMEM)


def call(kernel, outs, info, *args, loads=(), stores=(), scratch=(), on_chip=True):
    args = [pltpu.with_memory_space_constraint(x, pltpu.VMEM) for x in args]
    head = [] if info is None else [info]
    loads = [pltpu.with_memory_space_constraint(x, pltpu.HBM) for x in loads]
    apart = pl.BlockSpec(memory_space=pltpu.HBM)
    return pl.pallas_call(
        kernel,
        out_shape=[
            pltpu.VMEM(s, F32) if on_chip else jax.ShapeDtypeStruct(s, F32) for s in outs
        ] + [pltpu.HBM(s, F32) for s in stores],
        in_specs=[SMEM] * len(head) + [VMEM] * len(args) + [apart] * len(loads),
        out_specs=[VMEM] * len(outs) + [apart] * len(stores),
        scratch_shapes=list(scratch),
        compiler_params=pltpu.CompilerParams(vmem_limit_bytes=32 << 20),
    )(*head, *args, *loads)


EXT_SHAPE = (4, EXT + EXT // 2, WIN)
BAND = (4, EXT // 2, WIN)
HALF = (4, WIN, WIN)
PLACE = pltpu.VMEM((4, TALL, 2 * WIN), F32)
STEP_SCRATCH = (
    PLACE,
    PLACE,
    pltpu.VMEM((2 * MODES, WIN, WIN), F32),
    pltpu.VMEM((4, WIN, WIN), BF16),
    pltpu.VMEM((2, WIN, WIN), F32),
    pltpu.VMEM((WIN, WIN), F32),
)
SEMS = (pltpu.SemaphoreType.DMA((6,)),)
HELD = (pltpu.VMEM((2 * MODES, WIN, WIN), F32),)


def swap_near(x, axis):
    return lax.ppermute(x, axis, [(0, 1), (1, 0)])


def swap_far(x, axes, size):
    pairs = [(i, i + 1) for i in range(1, size - 1, 2)]
    return lax.ppermute(x, axes, pairs + [(j, i) for i, j in pairs])


def rows_swapped(near, far):
    return swap_near(near, "core"), swap_far(far, ROW, N_ROW)


def cols_swapped(near, far):
    return swap_near(near, "xl"), swap_far(far, COL, N_COL)


def swap_cores(x):
    return lax.ppermute(x, "core", [(0, 1), (1, 0)])


def chip_exchange(x):
    return lax.all_to_all(x, CHIPS, 0, 0, tiled=True)


def join_kernel(keep, other, out):
    out[...] = keep[...] + other[...]


def spread_kernel(parts, out):
    total = jnp.sum(parts[...].reshape(-1, 8, WIN), axis=0)
    total = total + pltpu.roll(total, 4, 0)
    out[...] = jnp.broadcast_to(total[None], (HALF[0] * WIN // 8, 8, WIN)).reshape(HALF)


def summed_half(keep, send):
    (total,) = call(join_kernel, [HALF], None, keep, swap_cores(send))
    parts = chip_exchange(total.reshape(N_CHIPS, -1, WIN)).reshape(HALF)
    (spread,) = call(spread_kernel, [HALF], None, parts)
    return chip_exchange(spread.reshape(N_CHIPS, -1, WIN)).reshape(HALF)


def exchanged(info, grad, near, far, b):
    rows = rows_swapped(near, far)
    near, far = call(
        lambda *refs: middle_kernel(b, *refs), [BAND, BAND], info, grad, *rows,
        scratch=(PLACE,),
    )
    return grad, *rows, *cols_swapped(near, far)


def steps(object_field, probe, kernel_phase, amplitudes, offsets):
    rate = PROBE_RATE / math.sqrt(N_ROW * N_COL)
    tables = jnp.asarray(dft_tables())
    kcos, ksin = jnp.cos(kernel_phase), jnp.sin(kernel_phase)
    row = lax.axis_index(ROW)
    col = lax.axis_index(COL)
    core = lax.axis_index("core")
    edges = jnp.stack([
        jnp.where(row == 0, OVL, 0),
        jnp.where(row == N_ROW - 1, EXT - OVL, EXT),
        jnp.where(col == 0, OVL, 0),
        jnp.where(col == N_COL - 1, EXT - OVL, EXT),
        core,
        lax.axis_index("xl"),
    ]).astype(jnp.int32)
    info = jnp.concatenate([offsets.reshape(-1), edges])
    measured = amplitudes[:, 0, 0]
    obj = object_field.reshape(4, WIN, WIN)
    probe = probe.reshape(2 * MODES, WIN, WIN)
    loads = (probe, tables, kcos, ksin, measured)

    rows = call(cut_kernel, [(4, OVL, WIN)] * 2, edges, obj)
    rows = rows_swapped(*rows)
    cols = call(halo_kernel, [(4, 48, WIN)] * 2, info, obj, *rows)
    cols = cols_swapped(*cols)

    step_outs = [EXT_SHAPE, HALF, BAND, BAND]
    whole = (2 * MODES, WIN, WIN)
    extended, grad, near, far, keep0, send0 = call(
        first_kernel, step_outs + [HALF, HALF], info, obj, *rows, *cols,
        loads=loads, scratch=STEP_SCRATCH + SEMS,
    )
    moves = exchanged(info, grad, near, far, 0)
    mine0 = summed_half(keep0, send0)
    other0 = swap_cores(mine0)
    extended, grad, near, far, held = call(
        second_kernel, step_outs, info, extended, *moves,
        loads=loads, stores=(whole,), scratch=STEP_SCRATCH + HELD + SEMS,
    )
    moves = exchanged(info, grad, near, far, 1)
    own, grad, near, far, keep2, send2, probe = call(
        lambda *refs: third_kernel(rate, *refs), [HALF] + step_outs[1:] + [HALF, HALF, whole],
        info, extended, *moves, mine0, other0,
        loads=loads + (held,), scratch=STEP_SCRATCH + HELD + SEMS,
    )
    moves = exchanged(info, grad, near, far, 2)
    mine = summed_half(keep2, send2)
    other = swap_cores(mine)
    (obj,) = call(object_kernel, [HALF], info, own, *moves, scratch=(PLACE,), on_chip=False)
    (probe,) = call(
        lambda *refs: update_probe(rate, *refs), [(2 * MODES, WIN, WIN)],
        info, probe, mine, other, on_chip=False,
    )
    return obj.reshape(2, 2, WIN, WIN), probe.reshape(MODES, 2, WIN, WIN)


def solution(mesh):
    fine = Mesh(mesh.devices.reshape(SIZES), AXES)
    in_specs = (
        P(None, None, ROW, COL),
        P(),
        P(),
        P(None, ROW, COL, None, None),
        P(None, ROW, COL, None),
    )
    out_specs = (P(None, None, ROW, COL), P())
    return jax.shard_map(steps, mesh=fine, in_specs=in_specs, out_specs=out_specs, check_vma=False)
```

```python
import math

import jax
import jax.numpy as jnp
import numpy as np
from jax import lax
from jax.experimental import pallas as pl
from jax.experimental.pallas import tpu as pltpu
from jax.sharding import Mesh, PartitionSpec as P


WIN = 128
OVL = 32
EXT = WIN + 2 * OVL
TALL = EXT + 8
MODES = 4
OBJECT_RATE = 0.5
PROBE_RATE = 0.5
FLOOR = 0.1

AXES = ("z", "xh", "core", "y", "xl")
SIZES = (8, 2, 2, 4, 2)
ROW = ("z", "xh", "core")
COL = ("y", "xl")
CHIPS = ("z", "xh", "y", "xl")
N_ROW = 32
N_COL = 8
N_CHIPS = 128
CORE = 10
XLOW = 11

F32 = jnp.float32
BF16 = jnp.bfloat16


def dft_tables():
    counter = np.arange(WIN, dtype=np.int64)
    phase = (counter[:, None] * counter[None, :] % WIN).astype(np.float64) * (-2.0 * math.pi / WIN)
    out = []
    for table in (np.cos(phase) / math.sqrt(WIN), np.sin(phase) / math.sqrt(WIN)):
        high = table.astype(np.float32).astype(jnp.bfloat16)
        low = (table - high.astype(np.float64)).astype(np.float32).astype(jnp.bfloat16)
        out += [high, low]
    return np.stack(out)


def full_tables(refs):
    out = []
    for part in range(2):
        cosine, sine = refs[part], refs[2 + part]
        out.append(grid_of([[cosine, sine], [-sine, cosine]]))
        out.append(grid_of([[cosine, -sine], [sine, cosine]]))
    return out


def lanes(shape):
    return lax.broadcasted_iota(jnp.int32, shape, len(shape) - 1)


def split(x):
    high = x.astype(BF16)
    return high, (x - high.astype(F32)).astype(BF16)


def dot(a, b):
    return lax.dot_general(a, b, (((1,), (0,)), ((), ())), preferred_element_type=F32)


def grid_of(blocks):
    return jnp.concatenate([jnp.concatenate(line, axis=1) for line in blocks], axis=0)


def blocks_of(x):
    half = WIN
    return [[x[:half, :half], x[:half, half:]], [x[half:, :half], x[half:, half:]]]


def transposed(blocks):
    return [[blocks[0][0], blocks[1][0]], [blocks[0][1], blocks[1][1]]]


def apply_right(pairs, high, low):
    out = []
    for blocks in pairs:
        xh, xl = split(grid_of(blocks))
        out.append(blocks_of(dot(xh, high) + dot(xh, low) + dot(xl, high)))
    return out


def apply_left(pairs, high, low):
    out = []
    for blocks in pairs:
        xh, xl = split(grid_of(transposed(blocks)))
        out.append(transposed(blocks_of(dot(high, xh) + dot(low, xh) + dot(high, xl))))
    return out


def product(a, b):
    return [a[0] * b[0] - a[1] * b[1], a[0] * b[1] + a[1] * b[0]]


def conj_product(a, b):
    return [a[0] * b[0] + a[1] * b[1], a[0] * b[1] - a[1] * b[0]]


def per_mode(pairs, fn):
    return [[fn(pairs[m // 2][m % 2], m) for m in (2 * k, 2 * k + 1)] for k in range(2)]


def rows_up(rows, by):
    groups = rows.reshape(-1, 8, WIN)
    turned = pltpu.roll(groups, (8 - by) % 8, 1)
    line = lax.broadcasted_iota(jnp.int32, (WIN // 8, 8, WIN), 1)
    return jnp.where(line < 8 - by, turned[:-1], turned[1:]).reshape(WIN, WIN)


def rows_down(rows, by):
    groups = rows.reshape(-1, 8, WIN)
    turned = pltpu.roll(groups, by, 1)
    zero = jnp.zeros((1, 8, WIN), F32)
    line = lax.broadcasted_iota(jnp.int32, (WIN // 8 + 1, 8, WIN), 1)
    first = jnp.concatenate([turned, zero], axis=0)
    second = jnp.concatenate([zero, turned], axis=0)
    return jnp.where(line >= by, first, second).reshape(WIN + 8, WIN)


def place_window(e_ref, oy, ox, which):
    base = pl.multiple_of(oy // 8 * 8, 8)
    back = (WIN - ox) % WIN
    parts = []
    for t in range(2):
        rows = e_ref[which, pl.ds(base, WIN + 8), t * WIN : (t + 1) * WIN]
        parts.append(pltpu.roll(rows_up(rows, oy % 8), back, 1))
    first, second = parts
    return jnp.where(lanes((WIN, WIN)) < WIN - ox, first, second)


def pack_cols(tile):
    half = EXT // 2
    lane = lanes((half, WIN))
    return jnp.where(lane < 64, tile[:half], pltpu.roll(tile[half:], 64, 1))


def unpack_cols(packed):
    low = lanes(packed.shape) < 64
    return jnp.concatenate(
        [jnp.where(low, packed, 0.0), jnp.where(low, pltpu.roll(packed, 64, 1), 0.0)], axis=0
    )


def pack_rows(first, second):
    lane = lanes((32, WIN))
    rest = jnp.where(lane < 64, second[:32], pltpu.roll(second[32:], 64, 1))
    return jnp.concatenate([first, rest], axis=0)


def unpack_rows(packed):
    rest = packed[64:]
    low = lanes(rest.shape) < 64
    second = jnp.concatenate(
        [jnp.where(low, rest, 0.0), jnp.where(low, pltpu.roll(rest, 64, 1), 0.0)], axis=0
    )
    return packed[:64], second


def by_parity(odd, pair, near, far, a):
    first, last = pair
    near[a] = jnp.where(odd, first, last)
    far[a] = jnp.where(odd, last, first)


def sides(odd, near, far, a):
    return jnp.where(odd, near[a], far[a]), jnp.where(odd, far[a], near[a])


def cut_kernel(info, obj, near, far, sem):
    edge = WIN - OVL
    odd = info[CORE - 6]
    copies = [
        pltpu.make_async_copy(obj.at[:, pl.ds(pl.multiple_of(start * edge, 8), OVL), :], out, sem.at[i])
        for i, (start, out) in enumerate(((1 - odd, near), (odd, far)))
    ]
    for copy in copies:
        copy.start()
    for copy in copies:
        copy.wait()


def halo_kernel(info, obj, row_near, row_far, near, far):
    lane = lanes((48, WIN)) // 32
    for a in range(4):
        north, south = sides(info[CORE] == 1, row_near, row_far, a)
        column = jnp.concatenate([north, obj[a], south], axis=0)
        strips = []
        for base in (0, 32):
            out = jnp.zeros((48, WIN), F32)
            for i in range(4):
                part = column[48 * i : 48 * i + 48]
                shift = (32 * i + base) % WIN
                part = pltpu.roll(part, shift, 1) if shift else part
                out = jnp.where(lane == i, part, out)
            strips.append(out)
        by_parity(info[XLOW] == 1, strips, near, far, a)


def build_extended(e_ref, info, obj, row_near, row_far, col_near, col_far):
    lane = lanes((EXT, WIN))
    for a in range(4):
        north, south = sides(info[CORE] == 1, row_near, row_far, a)
        west, east = sides(info[XLOW] == 1, col_near, col_far, a)
        column = jnp.concatenate([north, obj[a], south], axis=0)
        column = pltpu.roll(column, 32, 1)
        lefts, rights = [], []
        for i in range(4):
            shift = (WIN - 32 * i) % WIN
            lefts.append(pltpu.roll(west, shift, 1) if shift else west)
            shift = (32 - 32 * i) % WIN
            rights.append(pltpu.roll(east, shift, 1) if shift else east)
        e_ref[a, :EXT, :WIN] = jnp.where(lane < 32, jnp.concatenate(lefts, axis=0), column)
        e_ref[a, :EXT, WIN:] = jnp.where(
            lane < 32, column, jnp.where(lane < 64, jnp.concatenate(rights, axis=0), 0.0)
        )


def place_gradient(info, b, grads, g_ref):
    oy, ox = info[2 * b], info[2 * b + 1]
    lane = lanes((WIN + 8, WIN))
    base = pl.multiple_of(oy // 8 * 8, 8)
    for a in range(4):
        g_ref[a] = jnp.zeros((TALL, 2 * WIN), F32)
        turned = rows_down(pltpu.roll(grads[a], ox, 1), oy % 8)
        for t in range(2):
            part = jnp.where(lane >= ox if t == 0 else lane < ox, turned, 0.0)
            g_ref[a, pl.ds(base, WIN + 8), t * WIN : (t + 1) * WIN] = part


def total_gradient(info, g_ref, cols, rows, a):
    west_east = sides(info[XLOW] == 1, *cols, a)
    north, south = (unpack_rows(x) for x in sides(info[CORE] == 1, *rows, a))
    gap = jnp.zeros((64, WIN), F32)
    out = []
    for t in range(2):
        bands = jnp.concatenate([north[t], gap, south[t]], axis=0)
        own = g_ref[a, :EXT, t * WIN : (t + 1) * WIN]
        out.append(own + unpack_cols(west_east[t]) + bands)
    return out


def pack_extended(e_ref, out):
    for a in range(4):
        out[a, :EXT] = e_ref[a, :EXT, :WIN]
        out[a, EXT:] = pack_cols(e_ref[a, :EXT, WIN:])


def own_part(parts):
    lane = lanes((WIN, WIN))
    turned = [pltpu.roll(x[OVL : OVL + WIN], WIN - OVL, 1) for x in parts]
    return jnp.where(lane < WIN - OVL, turned[0], turned[1])


def update_extended(e_ref, g_ref, info, b, old, grads, cols, rows):
    place_gradient(info, b - 1, grads, g_ref)
    row = lax.broadcasted_iota(jnp.int32, (EXT, WIN), 0)
    lane = lanes((EXT, WIN))
    in_rows = (row >= info[6]) & (row < info[7])
    keep = (in_rows & (lane >= info[8]), in_rows & (lane + WIN < info[9]))
    for a in range(4):
        grad = total_gradient(info, g_ref, cols, rows, a)
        before = (old[a, :EXT], unpack_cols(old[a, EXT:]))
        for t in range(2):
            value = before[t] - OBJECT_RATE * grad[t]
            e_ref[a, :EXT, t * WIN : (t + 1) * WIN] = jnp.where(keep[t], value, 0.0)


def step_core(info, b, e_ref, probe, loads, kernel, measured, tables, g_ref, w_ref, near, far):
    oy, ox = info[2 * b], info[2 * b + 1]
    o1 = [place_window(e_ref, oy, ox, 0), place_window(e_ref, oy, ox, 1)]
    o2 = [place_window(e_ref, oy, ox, 2), place_window(e_ref, oy, ox, 3)]
    loads[1].wait()
    a_high, b_high, a_low, b_low = full_tables(tables)
    x = per_mode(probe, lambda p, m: product(p, o1))
    for load in loads[2:]:
        load.wait()
    phase = [kernel[0], kernel[1]]
    x = apply_left(apply_right(x, a_high, a_low), b_high, b_low)
    x = per_mode(x, lambda v, m: product(phase, v))
    phi = apply_right(apply_left(x, a_high, a_low), b_high, b_low)
    x = per_mode(phi, lambda v, m: product(v, o2))
    x = apply_left(apply_right(x, a_high, a_low), b_high, b_low)
    intensity = sum(x[m // 2][m % 2][c] * x[m // 2][m % 2][c] for m in range(MODES) for c in range(2))
    factor = 1.0 - measured[...] / jnp.sqrt(intensity + FLOOR)
    x = per_mode(x, lambda v, m: [v[0] * factor, v[1] * factor])
    chi2 = apply_right(apply_left(x, a_high, a_low), b_high, b_low)
    terms2 = [conj_product(phi[m // 2][m % 2], chi2[m // 2][m % 2]) for m in range(MODES)]
    x = per_mode(chi2, lambda v, m: conj_product(o2, v))
    x = apply_left(apply_right(x, a_high, a_low), b_high, b_low)
    x = per_mode(x, lambda v, m: conj_product(phase, v))
    chi1 = apply_right(apply_left(x, a_high, a_low), b_high, b_low)
    terms1 = [conj_product(probe[m // 2][m % 2], chi1[m // 2][m % 2]) for m in range(MODES)]
    grads = [sum(t[c] for t in terms1) for c in range(2)] + [sum(t[c] for t in terms2) for c in range(2)]
    for a in range(4):
        w_ref[a] = grads[a]
    place_gradient(info, b, grads, g_ref)
    for a in range(4):
        first, second = g_ref[a, :EXT, :WIN], g_ref[a, :EXT, WIN:]
        if b < 2:
            strips = (pack_cols(first), pack_cols(second))
        else:
            strips = (pack_strip(first, 0), pack_strip(second, OVL))
        by_parity(info[XLOW] == 1, strips, near, far, a)
    return per_mode(chi1, lambda v, m: conj_product(o1, v))


def probe_blocks(probe_ref):
    return [[[probe_ref[2 * m], probe_ref[2 * m + 1]] for m in (2 * k, 2 * k + 1)] for k in range(2)]


def write_halves(info, grads, keep, send):
    first = info[CORE] == 0
    for i in range(4):
        low = grads[0][i // 2][i % 2]
        high = grads[1][i // 2][i % 2]
        keep[i] = jnp.where(first, low, high)
        send[i] = jnp.where(first, high, low)


def loads_of(b, probe, tables, kcos, ksin, measured, p_s, t_s, k_s, m_s, sem):
    pairs = (
        (probe, p_s), (tables, t_s), (kcos, k_s.at[0]), (ksin, k_s.at[1]), (measured.at[b], m_s)
    )
    copies = [pltpu.make_async_copy(x, y, sem.at[i]) for i, (x, y) in enumerate(pairs)]
    for copy in copies:
        copy.start()
    return copies


def first_kernel(info, obj, row_near, row_far, col_near, col_far, probe, tables, kcos, ksin, measured,
                 e_out, w_ref, near, far, keep, send, e_s, g_s, p_s, t_s, k_s, m_s, sem):
    loads = loads_of(0, probe, tables, kcos, ksin, measured, p_s, t_s, k_s, m_s, sem)
    build_extended(e_s, info, obj, row_near, row_far, col_near, col_far)
    pack_extended(e_s, e_out)
    loads[0].wait()
    grads = step_core(info, 0, e_s, probe_blocks(p_s), loads, k_s, m_s, t_s, g_s, w_ref, near, far)
    write_halves(info, grads, keep, send)


def second_kernel(info, old, grad, cn, cf, rn, rf, probe, tables, kcos, ksin, measured,
                  e_out, w_ref, near, far, held, e_s, g_s, p_s, t_s, k_s, m_s, h_s, sem):
    loads = loads_of(1, probe, tables, kcos, ksin, measured, p_s, t_s, k_s, m_s, sem)
    update_extended(e_s, g_s, info, 1, old, grad, (cn, cf), (rn, rf))
    pack_extended(e_s, e_out)
    loads[0].wait()
    grads = step_core(info, 1, e_s, probe_blocks(p_s), loads, k_s, m_s, t_s, g_s, w_ref, near, far)
    for m in range(MODES):
        h_s[2 * m] = grads[m // 2][m % 2][0]
        h_s[2 * m + 1] = grads[m // 2][m % 2][1]
    store = pltpu.make_async_copy(h_s, held, sem.at[5])
    store.start()
    store.wait()


def third_kernel(rate, info, old, grad, cn, cf, rn, rf, mine, other,
                 probe, tables, kcos, ksin, measured, held,
                 own, w_ref, near, far, keep, send, p_out, e_s, g_s, p_s, t_s, k_s, m_s, h_s, sem):
    loads = loads_of(2, probe, tables, kcos, ksin, measured, p_s, t_s, k_s, m_s, sem)
    load_held = pltpu.make_async_copy(held, h_s, sem.at[5])
    load_held.start()
    update_extended(e_s, g_s, info, 2, old, grad, (cn, cf), (rn, rf))
    for a in range(4):
        own[a] = own_part((e_s[a, :, :WIN], e_s[a, :, WIN:]))
    loads[0].wait()
    update_probe(rate, info, p_s, mine, other, p_out)
    grads = step_core(info, 2, e_s, probe_blocks(p_out), loads, k_s, m_s, t_s, g_s, w_ref, near, far)
    load_held.wait()
    grads = per_mode(grads, lambda v, m: [v[c] + h_s[2 * m + c] for c in range(2)])
    write_halves(info, grads, keep, send)


def update_probe(rate, info, probe, mine, other, out):
    first = info[CORE] == 0
    for i in range(4):
        out[i] = probe[i] - rate * jnp.where(first, mine[i], other[i])
        out[4 + i] = probe[4 + i] - rate * jnp.where(first, other[i], mine[i])


def middle_kernel(b, info, grad, cn, cf, near, far, g_s):
    place_gradient(info, b, grad, g_s)
    for a in range(4):
        west_east = [unpack_cols(x) for x in sides(info[XLOW] == 1, cn, cf, a)]
        full = [g_s[a, :EXT, t * WIN : (t + 1) * WIN] + west_east[t] for t in range(2)]
        up = pack_rows(full[0][:64], full[1][:64])
        down = pack_rows(full[0][128:], full[1][128:])
        by_parity(info[CORE] == 1, (up, down), near, far, a)


def pack_strip(column, lane):
    group = lanes((EXT // 4, WIN)) // OVL
    out = jnp.zeros((EXT // 4, WIN), F32)
    for i in range(4):
        part = pltpu.roll(column[EXT // 4 * i : EXT // 4 * (i + 1)], (OVL * i - lane) % WIN, 1)
        out = jnp.where(group == i, part, out)
    return out


def unpack_strip(packed, lane):
    parts = [pltpu.roll(packed, (lane - OVL * i) % WIN, 1) for i in range(4)]
    column = jnp.concatenate(parts, axis=0)
    return jnp.where(lanes(column.shape) // OVL == lane // OVL, column, 0.0)


def last_middle_kernel(info, grad, cn, cf, near, far, center, g_s):
    place_gradient(info, 2, grad, g_s)
    lane = lanes((EXT, WIN))
    for a in range(4):
        west, east = sides(info[XLOW] == 1, cn, cf, a)
        turned = [pltpu.roll(g_s[a, :EXT, t * WIN : (t + 1) * WIN], WIN - OVL, 1) for t in range(2)]
        full = jnp.where(lane < WIN - OVL, turned[0], turned[1])
        full = full + unpack_strip(west, 0) + unpack_strip(east, WIN - OVL)
        center[a] = full[OVL : OVL + WIN]
        by_parity(info[CORE] == 1, (full[:OVL], full[OVL + WIN :]), near, far, a)


def object_kernel(info, own, center, rn, rf, out):
    for a in range(4):
        north, south = sides(info[CORE] == 1, rn, rf, a)
        bands = jnp.concatenate([north, jnp.zeros((WIN - 2 * OVL, WIN), F32), south], axis=0)
        out[a] = own[a] - OBJECT_RATE * (center[a] + bands)


SMEM = pl.BlockSpec(memory_space=pltpu.SMEM)
VMEM = pl.BlockSpec(memory_space=pltpu.VMEM)


def call(kernel, outs, info, *args, loads=(), stores=(), scratch=(), on_chip=True):
    args = [pltpu.with_memory_space_constraint(x, pltpu.VMEM) for x in args]
    head = [] if info is None else [info]
    loads = [pltpu.with_memory_space_constraint(x, pltpu.HBM) for x in loads]
    apart = pl.BlockSpec(memory_space=pltpu.HBM)
    return pl.pallas_call(
        kernel,
        out_shape=[
            pltpu.VMEM(s, F32) if on_chip else jax.ShapeDtypeStruct(s, F32) for s in outs
        ] + [pltpu.HBM(s, F32) for s in stores],
        in_specs=[SMEM] * len(head) + [VMEM] * len(args) + [apart] * len(loads),
        out_specs=[VMEM] * len(outs) + [apart] * len(stores),
        scratch_shapes=list(scratch),
        compiler_params=pltpu.CompilerParams(vmem_limit_bytes=32 << 20),
    )(*head, *args, *loads)


EXT_SHAPE = (4, EXT + EXT // 2, WIN)
BAND = (4, EXT // 2, WIN)
STRIP = (4, EXT // 4, WIN)
EDGE = (4, OVL, WIN)
HALF = (4, WIN, WIN)
PLACE = pltpu.VMEM((4, TALL, 2 * WIN), F32)
STEP_SCRATCH = (
    PLACE,
    PLACE,
    pltpu.VMEM((2 * MODES, WIN, WIN), F32),
    pltpu.VMEM((4, WIN, WIN), BF16),
    pltpu.VMEM((2, WIN, WIN), F32),
    pltpu.VMEM((WIN, WIN), F32),
)
SEMS = (pltpu.SemaphoreType.DMA((6,)),)
HELD = (pltpu.VMEM((2 * MODES, WIN, WIN), F32),)


def swap_near(x, axis):
    return lax.ppermute(x, axis, [(0, 1), (1, 0)])


def swap_far(x, axes, size):
    pairs = [(i, i + 1) for i in range(1, size - 1, 2)]
    return lax.ppermute(x, axes, pairs + [(j, i) for i, j in pairs])


def rows_swapped(near, far):
    return swap_near(near, "core"), swap_far(far, ROW, N_ROW)


def cols_swapped(near, far):
    return swap_near(near, "xl"), swap_far(far, COL, N_COL)


def swap_cores(x):
    return lax.ppermute(x, "core", [(0, 1), (1, 0)])


def chip_exchange(x):
    return lax.all_to_all(x, CHIPS, 0, 0, tiled=True)


def join_kernel(keep, other, out):
    out[...] = keep[...] + other[...]


def spread_kernel(parts, out):
    total = jnp.sum(parts[...].reshape(-1, 8, WIN), axis=0)
    total = total + pltpu.roll(total, 4, 0)
    out[...] = jnp.broadcast_to(total[None], (HALF[0] * WIN // 8, 8, WIN)).reshape(HALF)


def summed_half(keep, send):
    (total,) = call(join_kernel, [HALF], None, keep, swap_cores(send))
    parts = chip_exchange(total.reshape(N_CHIPS, -1, WIN)).reshape(HALF)
    (spread,) = call(spread_kernel, [HALF], None, parts)
    return chip_exchange(spread.reshape(N_CHIPS, -1, WIN)).reshape(HALF)


def exchanged(info, grad, near, far, b):
    cols = cols_swapped(near, far)
    near, far = call(
        lambda *refs: middle_kernel(b, *refs), [BAND, BAND], info, grad, *cols,
        scratch=(PLACE,),
    )
    return grad, *cols, *rows_swapped(near, far)


def steps(object_field, probe, kernel_phase, amplitudes, offsets):
    rate = PROBE_RATE / math.sqrt(N_ROW * N_COL)
    tables = jnp.asarray(dft_tables())
    kcos, ksin = jnp.cos(kernel_phase), jnp.sin(kernel_phase)
    row = lax.axis_index(ROW)
    col = lax.axis_index(COL)
    core = lax.axis_index("core")
    edges = jnp.stack([
        jnp.where(row == 0, OVL, 0),
        jnp.where(row == N_ROW - 1, EXT - OVL, EXT),
        jnp.where(col == 0, OVL, 0),
        jnp.where(col == N_COL - 1, EXT - OVL, EXT),
        core,
        lax.axis_index("xl"),
    ]).astype(jnp.int32)
    info = jnp.concatenate([offsets.reshape(-1), edges])
    measured = amplitudes[:, 0, 0]
    obj = object_field.reshape(4, WIN, WIN)
    probe = probe.reshape(2 * MODES, WIN, WIN)
    loads = (probe, tables, kcos, ksin, measured)

    rows = call(
        cut_kernel, [(4, OVL, WIN)] * 2, edges, loads=(obj,),
        scratch=(pltpu.SemaphoreType.DMA((2,)),),
    )
    rows = rows_swapped(*rows)
    cols = call(halo_kernel, [(4, 48, WIN)] * 2, info, obj, *rows)
    cols = cols_swapped(*cols)

    step_outs = [EXT_SHAPE, HALF, BAND, BAND]
    whole = (2 * MODES, WIN, WIN)
    extended, grad, near, far, keep0, send0 = call(
        first_kernel, step_outs + [HALF, HALF], info, obj, *rows, *cols,
        loads=loads, scratch=STEP_SCRATCH + SEMS,
    )
    moves = exchanged(info, grad, near, far, 0)
    mine0 = summed_half(keep0, send0)
    other0 = swap_cores(mine0)
    extended, grad, near, far, held = call(
        second_kernel, step_outs, info, extended, *moves,
        loads=loads, stores=(whole,), scratch=STEP_SCRATCH + HELD + SEMS,
    )
    moves = exchanged(info, grad, near, far, 1)
    own, grad, near, far, keep2, send2, probe = call(
        lambda *refs: third_kernel(rate, *refs), [HALF, HALF, STRIP, STRIP, HALF, HALF, whole],
        info, extended, *moves, mine0, other0,
        loads=loads + (held,), scratch=STEP_SCRATCH + HELD + SEMS,
    )
    cols = cols_swapped(near, far)
    near, far, center = call(
        last_middle_kernel, [EDGE, EDGE, HALF], info, grad, *cols, scratch=(PLACE,)
    )
    rows = rows_swapped(near, far)
    mine = summed_half(keep2, send2)
    other = swap_cores(mine)
    (obj,) = call(object_kernel, [HALF], info, own, center, *rows, on_chip=False)
    (probe,) = call(
        lambda *refs: update_probe(rate, *refs), [(2 * MODES, WIN, WIN)],
        info, probe, mine, other, on_chip=False,
    )
    return obj.reshape(2, 2, WIN, WIN), probe.reshape(MODES, 2, WIN, WIN)


def solution(mesh):
    fine = Mesh(mesh.devices.reshape(SIZES), AXES)
    in_specs = (
        P(None, None, ROW, COL),
        P(),
        P(),
        P(None, ROW, COL, None, None),
        P(None, ROW, COL, None),
    )
    out_specs = (P(None, None, ROW, COL), P())
    return jax.shard_map(steps, mesh=fine, in_specs=in_specs, out_specs=out_specs, check_vma=False)
```

```python
import math

import jax
import jax.numpy as jnp
import numpy as np
from jax import lax
from jax.experimental import pallas as pl
from jax.experimental.pallas import tpu as pltpu
from jax.sharding import Mesh, PartitionSpec as P


WIN = 128
OVL = 32
EXT = WIN + 2 * OVL
TALL = EXT + 8
MODES = 4
OBJECT_RATE = 0.5
PROBE_RATE = 0.5
FLOOR = 0.1

AXES = ("z", "xh", "core", "y", "xl")
SIZES = (8, 2, 2, 4, 2)
ROW = ("z", "xh", "core")
COL = ("y", "xl")
CHIPS = ("z", "xh", "y", "xl")
N_ROW = 32
N_COL = 8
N_CHIPS = 128
CORE = 10
XLOW = 11

F32 = jnp.float32
BF16 = jnp.bfloat16


def dft_tables():
    counter = np.arange(WIN, dtype=np.int64)
    phase = (counter[:, None] * counter[None, :] % WIN).astype(np.float64) * (-2.0 * math.pi / WIN)
    out = []
    for table in (np.cos(phase) / math.sqrt(WIN), np.sin(phase) / math.sqrt(WIN)):
        high = table.astype(np.float32).astype(jnp.bfloat16)
        low = (table - high.astype(np.float64)).astype(np.float32).astype(jnp.bfloat16)
        out += [high, low]
    return np.stack(out)


def full_tables(refs):
    out = []
    for part in range(2):
        cosine, sine = refs[part], refs[2 + part]
        out.append(grid_of([[cosine, sine], [-sine, cosine]]))
        out.append(grid_of([[cosine, -sine], [sine, cosine]]))
    return out


def lanes(shape):
    return lax.broadcasted_iota(jnp.int32, shape, len(shape) - 1)


def split(x):
    high = x.astype(BF16)
    return high, (x - high.astype(F32)).astype(BF16)


def dot(a, b):
    return lax.dot_general(a, b, (((1,), (0,)), ((), ())), preferred_element_type=F32)


def grid_of(blocks):
    return jnp.concatenate([jnp.concatenate(line, axis=1) for line in blocks], axis=0)


def blocks_of(x):
    half = WIN
    return [[x[:half, :half], x[:half, half:]], [x[half:, :half], x[half:, half:]]]


def transposed(blocks):
    return [[blocks[0][0], blocks[1][0]], [blocks[0][1], blocks[1][1]]]


def apply_right(pairs, high, low):
    out = []
    for blocks in pairs:
        xh, xl = split(grid_of(blocks))
        out.append(blocks_of(dot(xh, high) + dot(xh, low) + dot(xl, high)))
    return out


def apply_left(pairs, high, low):
    out = []
    for blocks in pairs:
        xh, xl = split(grid_of(transposed(blocks)))
        out.append(transposed(blocks_of(dot(high, xh) + dot(low, xh) + dot(high, xl))))
    return out


def product(a, b):
    return [a[0] * b[0] - a[1] * b[1], a[0] * b[1] + a[1] * b[0]]


def conj_product(a, b):
    return [a[0] * b[0] + a[1] * b[1], a[0] * b[1] - a[1] * b[0]]


def per_mode(pairs, fn):
    return [[fn(pairs[m // 2][m % 2], m) for m in (2 * k, 2 * k + 1)] for k in range(2)]


def rows_up(rows, by):
    groups = rows.reshape(-1, 8, WIN)
    turned = pltpu.roll(groups, (8 - by) % 8, 1)
    line = lax.broadcasted_iota(jnp.int32, (WIN // 8, 8, WIN), 1)
    return jnp.where(line < 8 - by, turned[:-1], turned[1:]).reshape(WIN, WIN)


def rows_down(rows, by):
    groups = rows.reshape(-1, 8, WIN)
    turned = pltpu.roll(groups, by, 1)
    zero = jnp.zeros((1, 8, WIN), F32)
    line = lax.broadcasted_iota(jnp.int32, (WIN // 8 + 1, 8, WIN), 1)
    first = jnp.concatenate([turned, zero], axis=0)
    second = jnp.concatenate([zero, turned], axis=0)
    return jnp.where(line >= by, first, second).reshape(WIN + 8, WIN)


def place_window(e_ref, oy, ox, which):
    base = pl.multiple_of(oy // 8 * 8, 8)
    back = (WIN - ox) % WIN
    parts = []
    for t in range(2):
        rows = e_ref[which, pl.ds(base, WIN + 8), t * WIN : (t + 1) * WIN]
        parts.append(pltpu.roll(rows_up(rows, oy % 8), back, 1))
    first, second = parts
    return jnp.where(lanes((WIN, WIN)) < WIN - ox, first, second)


def pack_cols(tile):
    half = EXT // 2
    lane = lanes((half, WIN))
    return jnp.where(lane < 64, tile[:half], pltpu.roll(tile[half:], 64, 1))


def unpack_cols(packed):
    low = lanes(packed.shape) < 64
    return jnp.concatenate(
        [jnp.where(low, packed, 0.0), jnp.where(low, pltpu.roll(packed, 64, 1), 0.0)], axis=0
    )


def pack_rows(first, second):
    lane = lanes((32, WIN))
    rest = jnp.where(lane < 64, second[:32], pltpu.roll(second[32:], 64, 1))
    return jnp.concatenate([first, rest], axis=0)


def unpack_rows(packed):
    rest = packed[64:]
    low = lanes(rest.shape) < 64
    second = jnp.concatenate(
        [jnp.where(low, rest, 0.0), jnp.where(low, pltpu.roll(rest, 64, 1), 0.0)], axis=0
    )
    return packed[:64], second


def by_parity(odd, pair, near, far, a):
    first, last = pair
    near[a] = jnp.where(odd, first, last)
    far[a] = jnp.where(odd, last, first)


def sides(odd, near, far, a):
    return jnp.where(odd, near[a], far[a]), jnp.where(odd, far[a], near[a])


def halo_kernel(info, obj, row_near, row_far, near, far):
    lane = lanes((48, WIN)) // 32
    for a in range(4):
        north, south = sides(info[CORE] == 1, row_near, row_far, a)
        column = jnp.concatenate([north, obj[a], south], axis=0)
        strips = []
        for base in (0, 32):
            out = jnp.zeros((48, WIN), F32)
            for i in range(4):
                part = column[48 * i : 48 * i + 48]
                shift = (32 * i + base) % WIN
                part = pltpu.roll(part, shift, 1) if shift else part
                out = jnp.where(lane == i, part, out)
            strips.append(out)
        by_parity(info[XLOW] == 1, strips, near, far, a)


def build_extended(e_ref, info, obj, row_near, row_far, col_near, col_far):
    lane = lanes((EXT, WIN))
    for a in range(4):
        north, south = sides(info[CORE] == 1, row_near, row_far, a)
        west, east = sides(info[XLOW] == 1, col_near, col_far, a)
        column = jnp.concatenate([north, obj[a], south], axis=0)
        column = pltpu.roll(column, 32, 1)
        lefts, rights = [], []
        for i in range(4):
            shift = (WIN - 32 * i) % WIN
            lefts.append(pltpu.roll(west, shift, 1) if shift else west)
            shift = (32 - 32 * i) % WIN
            rights.append(pltpu.roll(east, shift, 1) if shift else east)
        e_ref[a, :EXT, :WIN] = jnp.where(lane < 32, jnp.concatenate(lefts, axis=0), column)
        e_ref[a, :EXT, WIN:] = jnp.where(
            lane < 32, column, jnp.where(lane < 64, jnp.concatenate(rights, axis=0), 0.0)
        )


def place_gradient(info, b, grads, g_ref):
    oy, ox = info[2 * b], info[2 * b + 1]
    lane = lanes((WIN + 8, WIN))
    base = pl.multiple_of(oy // 8 * 8, 8)
    for a in range(4):
        g_ref[a] = jnp.zeros((TALL, 2 * WIN), F32)
        turned = rows_down(pltpu.roll(grads[a], ox, 1), oy % 8)
        for t in range(2):
            part = jnp.where(lane >= ox if t == 0 else lane < ox, turned, 0.0)
            g_ref[a, pl.ds(base, WIN + 8), t * WIN : (t + 1) * WIN] = part


def total_gradient(info, g_ref, cols, rows, a):
    west_east = sides(info[XLOW] == 1, *cols, a)
    north, south = (unpack_rows(x) for x in sides(info[CORE] == 1, *rows, a))
    gap = jnp.zeros((64, WIN), F32)
    out = []
    for t in range(2):
        bands = jnp.concatenate([north[t], gap, south[t]], axis=0)
        own = g_ref[a, :EXT, t * WIN : (t + 1) * WIN]
        out.append(own + unpack_cols(west_east[t]) + bands)
    return out


def pack_extended(e_ref, out):
    for a in range(4):
        out[a, :EXT] = e_ref[a, :EXT, :WIN]
        out[a, EXT:] = pack_cols(e_ref[a, :EXT, WIN:])


def own_part(parts):
    lane = lanes((WIN, WIN))
    turned = [pltpu.roll(x[OVL : OVL + WIN], WIN - OVL, 1) for x in parts]
    return jnp.where(lane < WIN - OVL, turned[0], turned[1])


def update_extended(e_ref, g_ref, info, b, old, grads, cols, rows):
    place_gradient(info, b - 1, grads, g_ref)
    row = lax.broadcasted_iota(jnp.int32, (EXT, WIN), 0)
    lane = lanes((EXT, WIN))
    in_rows = (row >= info[6]) & (row < info[7])
    keep = (in_rows & (lane >= info[8]), in_rows & (lane + WIN < info[9]))
    for a in range(4):
        grad = total_gradient(info, g_ref, cols, rows, a)
        before = (old[a, :EXT], unpack_cols(old[a, EXT:]))
        for t in range(2):
            value = before[t] - OBJECT_RATE * grad[t]
            e_ref[a, :EXT, t * WIN : (t + 1) * WIN] = jnp.where(keep[t], value, 0.0)


def step_core(info, b, e_ref, probe, loads, kernel, measured, tables, g_ref, w_ref, near, far):
    oy, ox = info[2 * b], info[2 * b + 1]
    o1 = [place_window(e_ref, oy, ox, 0), place_window(e_ref, oy, ox, 1)]
    o2 = [place_window(e_ref, oy, ox, 2), place_window(e_ref, oy, ox, 3)]
    loads[1].wait()
    a_high, b_high, a_low, b_low = full_tables(tables)
    x = per_mode(probe, lambda p, m: product(p, o1))
    for load in loads[2:]:
        load.wait()
    phase = [kernel[0], kernel[1]]
    x = apply_left(apply_right(x, a_high, a_low), b_high, b_low)
    x = per_mode(x, lambda v, m: product(phase, v))
    phi = apply_right(apply_left(x, a_high, a_low), b_high, b_low)
    x = per_mode(phi, lambda v, m: product(v, o2))
    x = apply_left(apply_right(x, a_high, a_low), b_high, b_low)
    intensity = sum(x[m // 2][m % 2][c] * x[m // 2][m % 2][c] for m in range(MODES) for c in range(2))
    factor = 1.0 - measured[...] / jnp.sqrt(intensity + FLOOR)
    x = per_mode(x, lambda v, m: [v[0] * factor, v[1] * factor])
    chi2 = apply_right(apply_left(x, a_high, a_low), b_high, b_low)
    terms2 = [conj_product(phi[m // 2][m % 2], chi2[m // 2][m % 2]) for m in range(MODES)]
    x = per_mode(chi2, lambda v, m: conj_product(o2, v))
    x = apply_left(apply_right(x, a_high, a_low), b_high, b_low)
    x = per_mode(x, lambda v, m: conj_product(phase, v))
    chi1 = apply_right(apply_left(x, a_high, a_low), b_high, b_low)
    terms1 = [conj_product(probe[m // 2][m % 2], chi1[m // 2][m % 2]) for m in range(MODES)]
    grads = [sum(t[c] for t in terms1) for c in range(2)] + [sum(t[c] for t in terms2) for c in range(2)]
    for a in range(4):
        w_ref[a] = grads[a]
    place_gradient(info, b, grads, g_ref)
    for a in range(4):
        first, second = g_ref[a, :EXT, :WIN], g_ref[a, :EXT, WIN:]
        if b < 2:
            strips = (pack_cols(first), pack_cols(second))
        else:
            strips = (pack_strip(first, 0), pack_strip(second, OVL))
        by_parity(info[XLOW] == 1, strips, near, far, a)
    return per_mode(chi1, lambda v, m: conj_product(o1, v))


def probe_blocks(probe_ref):
    return [[[probe_ref[2 * m], probe_ref[2 * m + 1]] for m in (2 * k, 2 * k + 1)] for k in range(2)]


def write_halves(info, grads, keep, send):
    first = info[CORE] == 0
    for i in range(4):
        low = grads[0][i // 2][i % 2]
        high = grads[1][i // 2][i % 2]
        keep[i] = jnp.where(first, low, high)
        send[i] = jnp.where(first, high, low)


def loads_of(b, probe, tables, kcos, ksin, measured, p_s, t_s, k_s, m_s, sem):
    pairs = (
        (probe, p_s), (tables, t_s), (kcos, k_s.at[0]), (ksin, k_s.at[1]), (measured.at[b], m_s)
    )
    copies = [pltpu.make_async_copy(x, y, sem.at[i]) for i, (x, y) in enumerate(pairs)]
    for copy in copies:
        copy.start()
    return copies


def first_kernel(info, obj, row_near, row_far, col_near, col_far, probe, tables, kcos, ksin, measured,
                 e_out, w_ref, near, far, keep, send, e_s, g_s, p_s, t_s, k_s, m_s, sem):
    loads = loads_of(0, probe, tables, kcos, ksin, measured, p_s, t_s, k_s, m_s, sem)
    build_extended(e_s, info, obj, row_near, row_far, col_near, col_far)
    pack_extended(e_s, e_out)
    loads[0].wait()
    grads = step_core(info, 0, e_s, probe_blocks(p_s), loads, k_s, m_s, t_s, g_s, w_ref, near, far)
    write_halves(info, grads, keep, send)


def second_kernel(info, old, grad, cn, cf, rn, rf, probe, tables, kcos, ksin, measured,
                  e_out, w_ref, near, far, held, e_s, g_s, p_s, t_s, k_s, m_s, h_s, sem):
    loads = loads_of(1, probe, tables, kcos, ksin, measured, p_s, t_s, k_s, m_s, sem)
    update_extended(e_s, g_s, info, 1, old, grad, (cn, cf), (rn, rf))
    pack_extended(e_s, e_out)
    loads[0].wait()
    grads = step_core(info, 1, e_s, probe_blocks(p_s), loads, k_s, m_s, t_s, g_s, w_ref, near, far)
    for m in range(MODES):
        h_s[2 * m] = grads[m // 2][m % 2][0]
        h_s[2 * m + 1] = grads[m // 2][m % 2][1]
    store = pltpu.make_async_copy(h_s, held, sem.at[5])
    store.start()
    store.wait()


def third_kernel(rate, info, old, grad, cn, cf, rn, rf, mine, other,
                 probe, tables, kcos, ksin, measured, held,
                 own, w_ref, near, far, keep, send, p_out, e_s, g_s, p_s, t_s, k_s, m_s, h_s, sem):
    loads = loads_of(2, probe, tables, kcos, ksin, measured, p_s, t_s, k_s, m_s, sem)
    load_held = pltpu.make_async_copy(held, h_s, sem.at[5])
    load_held.start()
    update_extended(e_s, g_s, info, 2, old, grad, (cn, cf), (rn, rf))
    for a in range(4):
        own[a] = own_part((e_s[a, :, :WIN], e_s[a, :, WIN:]))
    loads[0].wait()
    update_probe(rate, info, p_s, mine, other, p_out)
    grads = step_core(info, 2, e_s, probe_blocks(p_out), loads, k_s, m_s, t_s, g_s, w_ref, near, far)
    load_held.wait()
    grads = per_mode(grads, lambda v, m: [v[c] + h_s[2 * m + c] for c in range(2)])
    write_halves(info, grads, keep, send)


def update_probe(rate, info, probe, mine, other, out):
    first = info[CORE] == 0
    for i in range(4):
        out[i] = probe[i] - rate * jnp.where(first, mine[i], other[i])
        out[4 + i] = probe[4 + i] - rate * jnp.where(first, other[i], mine[i])


def middle_kernel(b, info, grad, cn, cf, near, far, g_s):
    place_gradient(info, b, grad, g_s)
    for a in range(4):
        west_east = [unpack_cols(x) for x in sides(info[XLOW] == 1, cn, cf, a)]
        full = [g_s[a, :EXT, t * WIN : (t + 1) * WIN] + west_east[t] for t in range(2)]
        up = pack_rows(full[0][:64], full[1][:64])
        down = pack_rows(full[0][128:], full[1][128:])
        by_parity(info[CORE] == 1, (up, down), near, far, a)


def pack_strip(column, lane):
    group = lanes((EXT // 4, WIN)) // OVL
    out = jnp.zeros((EXT // 4, WIN), F32)
    for i in range(4):
        part = pltpu.roll(column[EXT // 4 * i : EXT // 4 * (i + 1)], (OVL * i - lane) % WIN, 1)
        out = jnp.where(group == i, part, out)
    return out


def unpack_strip(packed, lane):
    parts = [pltpu.roll(packed, (lane - OVL * i) % WIN, 1) for i in range(4)]
    column = jnp.concatenate(parts, axis=0)
    return jnp.where(lanes(column.shape) // OVL == lane // OVL, column, 0.0)


def last_middle_kernel(info, grad, cn, cf, near, far, center, g_s):
    place_gradient(info, 2, grad, g_s)
    lane = lanes((EXT, WIN))
    for a in range(4):
        west, east = sides(info[XLOW] == 1, cn, cf, a)
        turned = [pltpu.roll(g_s[a, :EXT, t * WIN : (t + 1) * WIN], WIN - OVL, 1) for t in range(2)]
        full = jnp.where(lane < WIN - OVL, turned[0], turned[1])
        full = full + unpack_strip(west, 0) + unpack_strip(east, WIN - OVL)
        center[a] = full[OVL : OVL + WIN]
        by_parity(info[CORE] == 1, (full[:OVL], full[OVL + WIN :]), near, far, a)


def object_kernel(info, own, center, rn, rf, out):
    for a in range(4):
        north, south = sides(info[CORE] == 1, rn, rf, a)
        bands = jnp.concatenate([north, jnp.zeros((WIN - 2 * OVL, WIN), F32), south], axis=0)
        out[a] = own[a] - OBJECT_RATE * (center[a] + bands)


SMEM = pl.BlockSpec(memory_space=pltpu.SMEM)
VMEM = pl.BlockSpec(memory_space=pltpu.VMEM)


def call(kernel, outs, info, *args, loads=(), stores=(), scratch=(), on_chip=True):
    args = [pltpu.with_memory_space_constraint(x, pltpu.VMEM) for x in args]
    head = [] if info is None else [info]
    loads = [pltpu.with_memory_space_constraint(x, pltpu.HBM) for x in loads]
    apart = pl.BlockSpec(memory_space=pltpu.HBM)
    return pl.pallas_call(
        kernel,
        out_shape=[
            pltpu.VMEM(s, F32) if on_chip else jax.ShapeDtypeStruct(s, F32) for s in outs
        ] + [pltpu.HBM(s, F32) for s in stores],
        in_specs=[SMEM] * len(head) + [VMEM] * len(args) + [apart] * len(loads),
        out_specs=[VMEM] * len(outs) + [apart] * len(stores),
        scratch_shapes=list(scratch),
        compiler_params=pltpu.CompilerParams(vmem_limit_bytes=32 << 20),
    )(*head, *args, *loads)


EXT_SHAPE = (4, EXT + EXT // 2, WIN)
BAND = (4, EXT // 2, WIN)
STRIP = (4, EXT // 4, WIN)
EDGE = (4, OVL, WIN)
HALF = (4, WIN, WIN)
PLACE = pltpu.VMEM((4, TALL, 2 * WIN), F32)
STEP_SCRATCH = (
    PLACE,
    PLACE,
    pltpu.VMEM((2 * MODES, WIN, WIN), F32),
    pltpu.VMEM((4, WIN, WIN), BF16),
    pltpu.VMEM((2, WIN, WIN), F32),
    pltpu.VMEM((WIN, WIN), F32),
)
SEMS = (pltpu.SemaphoreType.DMA((6,)),)
HELD = (pltpu.VMEM((2 * MODES, WIN, WIN), F32),)


def swap_near(x, axis):
    return lax.ppermute(x, axis, [(0, 1), (1, 0)])


def swap_far(x, axes, size):
    pairs = [(i, i + 1) for i in range(1, size - 1, 2)]
    return lax.ppermute(x, axes, pairs + [(j, i) for i, j in pairs])


def rows_swapped(near, far):
    return swap_near(near, "core"), swap_far(far, ROW, N_ROW)


def cols_swapped(near, far):
    return swap_near(near, "xl"), swap_far(far, COL, N_COL)


def swap_cores(x):
    return lax.ppermute(x, "core", [(0, 1), (1, 0)])


def chip_exchange(x):
    return lax.all_to_all(x, CHIPS, 0, 0, tiled=True)


def join_kernel(keep, other, out):
    out[...] = keep[...] + other[...]


def spread_kernel(parts, out):
    total = jnp.sum(parts[...].reshape(-1, 8, WIN), axis=0)
    total = total + pltpu.roll(total, 4, 0)
    out[...] = jnp.broadcast_to(total[None], (HALF[0] * WIN // 8, 8, WIN)).reshape(HALF)


def summed_half(keep, send):
    (total,) = call(join_kernel, [HALF], None, keep, swap_cores(send))
    parts = chip_exchange(total.reshape(N_CHIPS, -1, WIN)).reshape(HALF)
    (spread,) = call(spread_kernel, [HALF], None, parts)
    return chip_exchange(spread.reshape(N_CHIPS, -1, WIN)).reshape(HALF)


def exchanged(info, grad, near, far, b):
    cols = cols_swapped(near, far)
    near, far = call(
        lambda *refs: middle_kernel(b, *refs), [BAND, BAND], info, grad, *cols,
        scratch=(PLACE,),
    )
    return grad, *cols, *rows_swapped(near, far)


def steps(object_field, probe, kernel_phase, amplitudes, offsets):
    rate = PROBE_RATE / math.sqrt(N_ROW * N_COL)
    tables = jnp.asarray(dft_tables())
    kcos, ksin = jnp.cos(kernel_phase), jnp.sin(kernel_phase)
    row = lax.axis_index(ROW)
    col = lax.axis_index(COL)
    core = lax.axis_index("core")
    edges = jnp.stack([
        jnp.where(row == 0, OVL, 0),
        jnp.where(row == N_ROW - 1, EXT - OVL, EXT),
        jnp.where(col == 0, OVL, 0),
        jnp.where(col == N_COL - 1, EXT - OVL, EXT),
        core,
        lax.axis_index("xl"),
    ]).astype(jnp.int32)
    info = jnp.concatenate([offsets.reshape(-1), edges])
    measured = amplitudes[:, 0, 0]
    obj = object_field.reshape(4, WIN, WIN)
    probe = probe.reshape(2 * MODES, WIN, WIN)
    loads = (probe, tables, kcos, ksin, measured)

    top, bottom = obj[:, :OVL], obj[:, WIN - OVL :]
    rows = jnp.where(core == 1, top, bottom), jnp.where(core == 1, bottom, top)
    rows = rows_swapped(*rows)
    cols = call(halo_kernel, [(4, 48, WIN)] * 2, info, obj, *rows)
    cols = cols_swapped(*cols)

    step_outs = [EXT_SHAPE, HALF, BAND, BAND]
    whole = (2 * MODES, WIN, WIN)
    extended, grad, near, far, keep0, send0 = call(
        first_kernel, step_outs + [HALF, HALF], info, obj, *rows, *cols,
        loads=loads, scratch=STEP_SCRATCH + SEMS,
    )
    moves = exchanged(info, grad, near, far, 0)
    mine0 = summed_half(keep0, send0)
    other0 = swap_cores(mine0)
    extended, grad, near, far, held = call(
        second_kernel, step_outs, info, extended, *moves,
        loads=loads, stores=(whole,), scratch=STEP_SCRATCH + HELD + SEMS,
    )
    moves = exchanged(info, grad, near, far, 1)
    own, grad, near, far, keep2, send2, probe = call(
        lambda *refs: third_kernel(rate, *refs), [HALF, HALF, STRIP, STRIP, HALF, HALF, whole],
        info, extended, *moves, mine0, other0,
        loads=loads + (held,), scratch=STEP_SCRATCH + HELD + SEMS,
    )
    cols = cols_swapped(near, far)
    near, far, center = call(
        last_middle_kernel, [EDGE, EDGE, HALF], info, grad, *cols, scratch=(PLACE,)
    )
    rows = rows_swapped(near, far)
    mine = summed_half(keep2, send2)
    other = swap_cores(mine)
    (obj,) = call(object_kernel, [HALF], info, own, center, *rows, on_chip=False)
    own_half = jnp.arange(2).reshape(2, 1, 1, 1) == core
    probe = probe.reshape(2, *HALF) - rate * jnp.where(own_half, mine, other)
    return obj.reshape(2, 2, WIN, WIN), probe.reshape(MODES, 2, WIN, WIN)


def solution(mesh):
    fine = Mesh(mesh.devices.reshape(SIZES), AXES)
    in_specs = (
        P(None, None, ROW, COL),
        P(),
        P(),
        P(None, ROW, COL, None, None),
        P(None, ROW, COL, None),
    )
    out_specs = (P(None, None, ROW, COL), P())
    return jax.shard_map(steps, mesh=fine, in_specs=in_specs, out_specs=out_specs, check_vma=False)
```

```python
import math

import jax
import jax.numpy as jnp
import numpy as np
from jax import lax
from jax.experimental import pallas as pl
from jax.experimental.pallas import tpu as pltpu
from jax.sharding import Mesh, PartitionSpec as P


WIN = 128
OVL = 32
EXT = WIN + 2 * OVL
TALL = EXT + 8
MODES = 4
OBJECT_RATE = 0.5
PROBE_RATE = 0.5
FLOOR = 0.1

AXES = ("z", "xh", "core", "y", "xl")
SIZES = (8, 2, 2, 4, 2)
ROW = ("z", "xh", "core")
COL = ("y", "xl")
CHIPS = ("z", "xh", "y", "xl")
N_ROW = 32
N_COL = 8
N_CHIPS = 128
CORE = 10
XLOW = 11

F32 = jnp.float32
BF16 = jnp.bfloat16


def dft_tables():
    counter = np.arange(WIN, dtype=np.int64)
    phase = (counter[:, None] * counter[None, :] % WIN).astype(np.float64) * (-2.0 * math.pi / WIN)
    out = []
    for table in (np.cos(phase) / math.sqrt(WIN), np.sin(phase) / math.sqrt(WIN)):
        high = table.astype(np.float32).astype(jnp.bfloat16)
        low = (table - high.astype(np.float64)).astype(np.float32).astype(jnp.bfloat16)
        out += [high, low]
    return np.stack(out)


def full_tables(refs):
    out = []
    for part in range(2):
        cosine, sine = refs[part], refs[2 + part]
        out.append(grid_of([[cosine, sine], [-sine, cosine]]))
        out.append(grid_of([[cosine, -sine], [sine, cosine]]))
    return out


def lanes(shape):
    return lax.broadcasted_iota(jnp.int32, shape, len(shape) - 1)


def split(x):
    high = x.astype(BF16)
    return high, (x - high.astype(F32)).astype(BF16)


def dot(a, b):
    return lax.dot_general(a, b, (((1,), (0,)), ((), ())), preferred_element_type=F32)


def grid_of(blocks):
    return jnp.concatenate([jnp.concatenate(line, axis=1) for line in blocks], axis=0)


def blocks_of(x):
    half = WIN
    return [[x[:half, :half], x[:half, half:]], [x[half:, :half], x[half:, half:]]]


def transposed(blocks):
    return [[blocks[0][0], blocks[1][0]], [blocks[0][1], blocks[1][1]]]


def apply_right(pairs, high, low):
    out = []
    for blocks in pairs:
        xh, xl = split(grid_of(blocks))
        out.append(blocks_of(dot(xh, high) + dot(xh, low) + dot(xl, high)))
    return out


def apply_left(pairs, high, low):
    out = []
    for blocks in pairs:
        xh, xl = split(grid_of(transposed(blocks)))
        out.append(transposed(blocks_of(dot(high, xh) + dot(low, xh) + dot(high, xl))))
    return out


def product(a, b):
    return [a[0] * b[0] - a[1] * b[1], a[0] * b[1] + a[1] * b[0]]


def conj_product(a, b):
    return [a[0] * b[0] + a[1] * b[1], a[0] * b[1] - a[1] * b[0]]


def per_mode(pairs, fn):
    return [[fn(pairs[m // 2][m % 2], m) for m in (2 * k, 2 * k + 1)] for k in range(2)]


def rows_up(rows, by):
    groups = rows.reshape(-1, 8, WIN)
    turned = pltpu.roll(groups, (8 - by) % 8, 1)
    line = lax.broadcasted_iota(jnp.int32, (WIN // 8, 8, WIN), 1)
    return jnp.where(line < 8 - by, turned[:-1], turned[1:]).reshape(WIN, WIN)


def rows_down(rows, by):
    groups = rows.reshape(-1, 8, WIN)
    turned = pltpu.roll(groups, by, 1)
    zero = jnp.zeros((1, 8, WIN), F32)
    line = lax.broadcasted_iota(jnp.int32, (WIN // 8 + 1, 8, WIN), 1)
    first = jnp.concatenate([turned, zero], axis=0)
    second = jnp.concatenate([zero, turned], axis=0)
    return jnp.where(line >= by, first, second).reshape(WIN + 8, WIN)


def place_window(e_ref, oy, ox, which):
    base = pl.multiple_of(oy // 8 * 8, 8)
    back = (WIN - ox) % WIN
    parts = []
    for t in range(2):
        rows = e_ref[which, pl.ds(base, WIN + 8), t * WIN : (t + 1) * WIN]
        parts.append(pltpu.roll(rows_up(rows, oy % 8), back, 1))
    first, second = parts
    return jnp.where(lanes((WIN, WIN)) < WIN - ox, first, second)


def pack_cols(tile):
    half = EXT // 2
    lane = lanes((half, WIN))
    return jnp.where(lane < 64, tile[:half], pltpu.roll(tile[half:], 64, 1))


def unpack_cols(packed):
    low = lanes(packed.shape) < 64
    return jnp.concatenate(
        [jnp.where(low, packed, 0.0), jnp.where(low, pltpu.roll(packed, 64, 1), 0.0)], axis=0
    )


def pack_rows(first, second):
    lane = lanes((32, WIN))
    rest = jnp.where(lane < 64, second[:32], pltpu.roll(second[32:], 64, 1))
    return jnp.concatenate([first, rest], axis=0)


def unpack_rows(packed):
    rest = packed[64:]
    low = lanes(rest.shape) < 64
    second = jnp.concatenate(
        [jnp.where(low, rest, 0.0), jnp.where(low, pltpu.roll(rest, 64, 1), 0.0)], axis=0
    )
    return packed[:64], second


def by_parity(odd, pair, near, far, a):
    first, last = pair
    near[a] = jnp.where(odd, first, last)
    far[a] = jnp.where(odd, last, first)


def sides(odd, near, far, a):
    return jnp.where(odd, near[a], far[a]), jnp.where(odd, far[a], near[a])


def halo_kernel(info, obj, row_near, row_far, near, far):
    lane = lanes((48, WIN)) // 32
    for a in range(4):
        north, south = sides(info[CORE] == 1, row_near, row_far, a)
        column = jnp.concatenate([north, obj[a], south], axis=0)
        strips = []
        for base in (0, 32):
            out = jnp.zeros((48, WIN), F32)
            for i in range(4):
                part = column[48 * i : 48 * i + 48]
                shift = (32 * i + base) % WIN
                part = pltpu.roll(part, shift, 1) if shift else part
                out = jnp.where(lane == i, part, out)
            strips.append(out)
        by_parity(info[XLOW] == 1, strips, near, far, a)


def build_extended(e_ref, info, obj, row_near, row_far, col_near, col_far):
    lane = lanes((EXT, WIN))
    for a in range(4):
        north, south = sides(info[CORE] == 1, row_near, row_far, a)
        west, east = sides(info[XLOW] == 1, col_near, col_far, a)
        column = jnp.concatenate([north, obj[a], south], axis=0)
        column = pltpu.roll(column, 32, 1)
        lefts, rights = [], []
        for i in range(4):
            shift = (WIN - 32 * i) % WIN
            lefts.append(pltpu.roll(west, shift, 1) if shift else west)
            shift = (32 - 32 * i) % WIN
            rights.append(pltpu.roll(east, shift, 1) if shift else east)
        e_ref[a, :EXT, :WIN] = jnp.where(lane < 32, jnp.concatenate(lefts, axis=0), column)
        e_ref[a, :EXT, WIN:] = jnp.where(
            lane < 32, column, jnp.where(lane < 64, jnp.concatenate(rights, axis=0), 0.0)
        )


def place_gradient(info, b, grads, g_ref):
    oy, ox = info[2 * b], info[2 * b + 1]
    lane = lanes((WIN + 8, WIN))
    base = pl.multiple_of(oy // 8 * 8, 8)
    for a in range(4):
        g_ref[a, :64] = jnp.zeros((64, 2 * WIN), F32)
        g_ref[a, WIN + 8 :] = jnp.zeros((64, 2 * WIN), F32)
        turned = rows_down(pltpu.roll(grads[a], ox, 1), oy % 8)
        for t in range(2):
            part = jnp.where(lane >= ox if t == 0 else lane < ox, turned, 0.0)
            g_ref[a, pl.ds(base, WIN + 8), t * WIN : (t + 1) * WIN] = part


def total_gradient(info, g_ref, cols, rows, a):
    west_east = sides(info[XLOW] == 1, *cols, a)
    north, south = (unpack_rows(x) for x in sides(info[CORE] == 1, *rows, a))
    gap = jnp.zeros((64, WIN), F32)
    out = []
    for t in range(2):
        bands = jnp.concatenate([north[t], gap, south[t]], axis=0)
        own = g_ref[a, :EXT, t * WIN : (t + 1) * WIN]
        out.append(own + unpack_cols(west_east[t]) + bands)
    return out


def pack_extended(e_ref, out):
    for a in range(4):
        out[a, :EXT] = e_ref[a, :EXT, :WIN]
        out[a, EXT:] = pack_cols(e_ref[a, :EXT, WIN:])


def own_part(parts):
    lane = lanes((WIN, WIN))
    turned = [pltpu.roll(x[OVL : OVL + WIN], WIN - OVL, 1) for x in parts]
    return jnp.where(lane < WIN - OVL, turned[0], turned[1])


def update_extended(e_ref, g_ref, info, b, old, grads, cols, rows):
    place_gradient(info, b - 1, grads, g_ref)
    row = lax.broadcasted_iota(jnp.int32, (EXT, WIN), 0)
    lane = lanes((EXT, WIN))
    in_rows = (row >= info[6]) & (row < info[7])
    keep = (in_rows & (lane >= info[8]), in_rows & (lane + WIN < info[9]))
    for a in range(4):
        grad = total_gradient(info, g_ref, cols, rows, a)
        before = (old[a, :EXT], unpack_cols(old[a, EXT:]))
        for t in range(2):
            value = before[t] - OBJECT_RATE * grad[t]
            e_ref[a, :EXT, t * WIN : (t + 1) * WIN] = jnp.where(keep[t], value, 0.0)


def step_core(info, b, e_ref, probe, loads, kernel, measured, tables, g_ref, w_ref, near, far, edge=None):
    oy, ox = info[2 * b], info[2 * b + 1]
    o1 = [place_window(e_ref, oy, ox, 0), place_window(e_ref, oy, ox, 1)]
    o2 = [place_window(e_ref, oy, ox, 2), place_window(e_ref, oy, ox, 3)]
    loads[1].wait()
    a_high, b_high, a_low, b_low = full_tables(tables)
    x = per_mode(probe, lambda p, m: product(p, o1))
    for load in loads[2:]:
        load.wait()
    phase = [kernel[0], kernel[1]]
    x = apply_left(apply_right(x, a_high, a_low), b_high, b_low)
    x = per_mode(x, lambda v, m: product(phase, v))
    phi = apply_right(apply_left(x, a_high, a_low), b_high, b_low)
    x = per_mode(phi, lambda v, m: product(v, o2))
    x = apply_left(apply_right(x, a_high, a_low), b_high, b_low)
    intensity = sum(x[m // 2][m % 2][c] * x[m // 2][m % 2][c] for m in range(MODES) for c in range(2))
    factor = 1.0 - measured[...] / jnp.sqrt(intensity + FLOOR)
    x = per_mode(x, lambda v, m: [v[0] * factor, v[1] * factor])
    chi2 = apply_right(apply_left(x, a_high, a_low), b_high, b_low)
    terms2 = [conj_product(phi[m // 2][m % 2], chi2[m // 2][m % 2]) for m in range(MODES)]
    x = per_mode(chi2, lambda v, m: conj_product(o2, v))
    x = apply_left(apply_right(x, a_high, a_low), b_high, b_low)
    x = per_mode(x, lambda v, m: conj_product(phase, v))
    chi1 = apply_right(apply_left(x, a_high, a_low), b_high, b_low)
    terms1 = [conj_product(probe[m // 2][m % 2], chi1[m // 2][m % 2]) for m in range(MODES)]
    grads = [sum(t[c] for t in terms1) for c in range(2)] + [sum(t[c] for t in terms2) for c in range(2)]
    for a in range(4):
        w_ref[a] = grads[a]
    place_gradient(info, b, grads, g_ref)
    for a in range(4):
        first, second = g_ref[a, :EXT, :WIN], g_ref[a, :EXT, WIN:]
        if b < 2:
            edge[a, : EXT // 2] = pack_rows(first[:64], second[:64])
            edge[a, EXT // 2 :] = pack_rows(first[WIN:], second[WIN:])
            strips = (pack_cols(first), pack_cols(second))
        else:
            strips = (pack_strip(first, 0), pack_strip(second, OVL))
        by_parity(info[XLOW] == 1, strips, near, far, a)
    return per_mode(chi1, lambda v, m: conj_product(o1, v))


def probe_blocks(probe_ref):
    return [[[probe_ref[2 * m], probe_ref[2 * m + 1]] for m in (2 * k, 2 * k + 1)] for k in range(2)]


def write_halves(info, grads, keep, send):
    first = info[CORE] == 0
    for i in range(4):
        low = grads[0][i // 2][i % 2]
        high = grads[1][i // 2][i % 2]
        keep[i] = jnp.where(first, low, high)
        send[i] = jnp.where(first, high, low)


def loads_of(b, probe, tables, kcos, ksin, measured, p_s, t_s, k_s, m_s, sem):
    pairs = (
        (probe, p_s), (tables, t_s), (kcos, k_s.at[0]), (ksin, k_s.at[1]), (measured.at[b], m_s)
    )
    copies = [pltpu.make_async_copy(x, y, sem.at[i]) for i, (x, y) in enumerate(pairs)]
    for copy in copies:
        copy.start()
    return copies


def first_kernel(info, obj, row_near, row_far, col_near, col_far, probe, tables, kcos, ksin, measured,
                 e_out, w_ref, near, far, edge, keep, send, e_s, g_s, p_s, t_s, k_s, m_s, sem):
    loads = loads_of(0, probe, tables, kcos, ksin, measured, p_s, t_s, k_s, m_s, sem)
    build_extended(e_s, info, obj, row_near, row_far, col_near, col_far)
    pack_extended(e_s, e_out)
    loads[0].wait()
    grads = step_core(info, 0, e_s, probe_blocks(p_s), loads, k_s, m_s, t_s, g_s, w_ref, near, far, edge)
    write_halves(info, grads, keep, send)


def second_kernel(info, old, grad, cn, cf, rn, rf, probe, tables, kcos, ksin, measured,
                  e_out, w_ref, near, far, edge, held, e_s, g_s, p_s, t_s, k_s, m_s, h_s, sem):
    loads = loads_of(1, probe, tables, kcos, ksin, measured, p_s, t_s, k_s, m_s, sem)
    update_extended(e_s, g_s, info, 1, old, grad, (cn, cf), (rn, rf))
    pack_extended(e_s, e_out)
    loads[0].wait()
    grads = step_core(info, 1, e_s, probe_blocks(p_s), loads, k_s, m_s, t_s, g_s, w_ref, near, far, edge)
    for m in range(MODES):
        h_s[2 * m] = grads[m // 2][m % 2][0]
        h_s[2 * m + 1] = grads[m // 2][m % 2][1]
    store = pltpu.make_async_copy(h_s, held, sem.at[5])
    store.start()
    store.wait()


def third_kernel(rate, info, old, grad, cn, cf, rn, rf, mine, other,
                 probe, tables, kcos, ksin, measured, held,
                 own, w_ref, near, far, keep, send, p_out, e_s, g_s, p_s, t_s, k_s, m_s, h_s, sem):
    loads = loads_of(2, probe, tables, kcos, ksin, measured, p_s, t_s, k_s, m_s, sem)
    load_held = pltpu.make_async_copy(held, h_s, sem.at[5])
    load_held.start()
    update_extended(e_s, g_s, info, 2, old, grad, (cn, cf), (rn, rf))
    for a in range(4):
        own[a] = own_part((e_s[a, :, :WIN], e_s[a, :, WIN:]))
    loads[0].wait()
    update_probe(rate, info, p_s, mine, other, p_out)
    grads = step_core(info, 2, e_s, probe_blocks(p_out), loads, k_s, m_s, t_s, g_s, w_ref, near, far)
    load_held.wait()
    grads = per_mode(grads, lambda v, m: [v[c] + h_s[2 * m + c] for c in range(2)])
    write_halves(info, grads, keep, send)


def update_probe(rate, info, probe, mine, other, out):
    first = info[CORE] == 0
    for i in range(4):
        out[i] = probe[i] - rate * jnp.where(first, mine[i], other[i])
        out[4 + i] = probe[4 + i] - rate * jnp.where(first, other[i], mine[i])


def middle_kernel(info, edge, cn, cf, near, far):
    for a in range(4):
        tiles = [unpack_cols(x) for x in sides(info[XLOW] == 1, cn, cf, a)]
        up = edge[a, : EXT // 2] + pack_rows(tiles[0][:64], tiles[1][:64])
        down = edge[a, EXT // 2 :] + pack_rows(tiles[0][WIN:], tiles[1][WIN:])
        by_parity(info[CORE] == 1, (up, down), near, far, a)


def pack_strip(column, lane):
    group = lanes((EXT // 4, WIN)) // OVL
    out = jnp.zeros((EXT // 4, WIN), F32)
    for i in range(4):
        part = pltpu.roll(column[EXT // 4 * i : EXT // 4 * (i + 1)], (OVL * i - lane) % WIN, 1)
        out = jnp.where(group == i, part, out)
    return out


def unpack_strip(packed, lane):
    parts = [pltpu.roll(packed, (lane - OVL * i) % WIN, 1) for i in range(4)]
    column = jnp.concatenate(parts, axis=0)
    return jnp.where(lanes(column.shape) // OVL == lane // OVL, column, 0.0)


def last_middle_kernel(info, grad, cn, cf, near, far, center, g_s):
    place_gradient(info, 2, grad, g_s)
    lane = lanes((EXT, WIN))
    for a in range(4):
        west, east = sides(info[XLOW] == 1, cn, cf, a)
        turned = [pltpu.roll(g_s[a, :EXT, t * WIN : (t + 1) * WIN], WIN - OVL, 1) for t in range(2)]
        full = jnp.where(lane < WIN - OVL, turned[0], turned[1])
        full = full + unpack_strip(west, 0) + unpack_strip(east, WIN - OVL)
        center[a] = full[OVL : OVL + WIN]
        by_parity(info[CORE] == 1, (full[:OVL], full[OVL + WIN :]), near, far, a)


def object_kernel(info, own, center, rn, rf, out):
    for a in range(4):
        north, south = sides(info[CORE] == 1, rn, rf, a)
        bands = jnp.concatenate([north, jnp.zeros((WIN - 2 * OVL, WIN), F32), south], axis=0)
        out[a] = own[a] - OBJECT_RATE * (center[a] + bands)


SMEM = pl.BlockSpec(memory_space=pltpu.SMEM)
VMEM = pl.BlockSpec(memory_space=pltpu.VMEM)


def call(kernel, outs, info, *args, loads=(), stores=(), scratch=(), on_chip=True):
    args = [pltpu.with_memory_space_constraint(x, pltpu.VMEM) for x in args]
    head = [] if info is None else [info]
    loads = [pltpu.with_memory_space_constraint(x, pltpu.HBM) for x in loads]
    apart = pl.BlockSpec(memory_space=pltpu.HBM)
    return pl.pallas_call(
        kernel,
        out_shape=[
            pltpu.VMEM(s, F32) if on_chip else jax.ShapeDtypeStruct(s, F32) for s in outs
        ] + [pltpu.HBM(s, F32) for s in stores],
        in_specs=[SMEM] * len(head) + [VMEM] * len(args) + [apart] * len(loads),
        out_specs=[VMEM] * len(outs) + [apart] * len(stores),
        scratch_shapes=list(scratch),
        compiler_params=pltpu.CompilerParams(vmem_limit_bytes=32 << 20),
    )(*head, *args, *loads)


EXT_SHAPE = (4, EXT + EXT // 2, WIN)
BAND = (4, EXT // 2, WIN)
STRIP = (4, EXT // 4, WIN)
EDGE = (4, OVL, WIN)
HALF = (4, WIN, WIN)
PLACE = pltpu.VMEM((4, TALL, 2 * WIN), F32)
STEP_SCRATCH = (
    PLACE,
    PLACE,
    pltpu.VMEM((2 * MODES, WIN, WIN), F32),
    pltpu.VMEM((4, WIN, WIN), BF16),
    pltpu.VMEM((2, WIN, WIN), F32),
    pltpu.VMEM((WIN, WIN), F32),
)
SEMS = (pltpu.SemaphoreType.DMA((6,)),)
HELD = (pltpu.VMEM((2 * MODES, WIN, WIN), F32),)


def swap_near(x, axis):
    return lax.ppermute(x, axis, [(0, 1), (1, 0)])


def swap_far(x, axes, size):
    pairs = [(i, i + 1) for i in range(1, size - 1, 2)]
    return lax.ppermute(x, axes, pairs + [(j, i) for i, j in pairs])


def rows_swapped(near, far):
    return swap_near(near, "core"), swap_far(far, ROW, N_ROW)


def cols_swapped(near, far):
    return swap_near(near, "xl"), swap_far(far, COL, N_COL)


def swap_cores(x):
    return lax.ppermute(x, "core", [(0, 1), (1, 0)])


def chip_exchange(x):
    return lax.all_to_all(x, CHIPS, 0, 0, tiled=True)


def join_kernel(keep, other, out):
    out[...] = keep[...] + other[...]


def spread_kernel(parts, out):
    total = jnp.sum(parts[...].reshape(-1, 8, WIN), axis=0)
    total = total + pltpu.roll(total, 4, 0)
    out[...] = jnp.broadcast_to(total[None], (HALF[0] * WIN // 8, 8, WIN)).reshape(HALF)


def summed_half(keep, send):
    (total,) = call(join_kernel, [HALF], None, keep, swap_cores(send))
    parts = chip_exchange(total.reshape(N_CHIPS, -1, WIN)).reshape(HALF)
    (spread,) = call(spread_kernel, [HALF], None, parts)
    return chip_exchange(spread.reshape(N_CHIPS, -1, WIN)).reshape(HALF)


def exchanged(info, grad, near, far, edge):
    cols = cols_swapped(near, far)
    near, far = call(middle_kernel, [BAND, BAND], info, edge, *cols)
    return grad, *cols, *rows_swapped(near, far)


def steps(object_field, probe, kernel_phase, amplitudes, offsets):
    rate = PROBE_RATE / math.sqrt(N_ROW * N_COL)
    tables = jnp.asarray(dft_tables())
    kcos, ksin = jnp.cos(kernel_phase), jnp.sin(kernel_phase)
    row = lax.axis_index(ROW)
    col = lax.axis_index(COL)
    core = lax.axis_index("core")
    edges = jnp.stack([
        jnp.where(row == 0, OVL, 0),
        jnp.where(row == N_ROW - 1, EXT - OVL, EXT),
        jnp.where(col == 0, OVL, 0),
        jnp.where(col == N_COL - 1, EXT - OVL, EXT),
        core,
        lax.axis_index("xl"),
    ]).astype(jnp.int32)
    info = jnp.concatenate([offsets.reshape(-1), edges])
    measured = amplitudes[:, 0, 0]
    obj = object_field.reshape(4, WIN, WIN)
    probe = probe.reshape(2 * MODES, WIN, WIN)
    loads = (probe, tables, kcos, ksin, measured)

    top, bottom = obj[:, :OVL], obj[:, WIN - OVL :]
    rows = jnp.where(core == 1, top, bottom), jnp.where(core == 1, bottom, top)
    rows = rows_swapped(*rows)
    cols = call(halo_kernel, [(4, 48, WIN)] * 2, info, obj, *rows)
    cols = cols_swapped(*cols)

    step_outs = [EXT_SHAPE, HALF, BAND, BAND, (4, EXT, WIN)]
    whole = (2 * MODES, WIN, WIN)
    extended, grad, near, far, edge, keep0, send0 = call(
        first_kernel, step_outs + [HALF, HALF], info, obj, *rows, *cols,
        loads=loads, scratch=STEP_SCRATCH + SEMS,
    )
    moves = exchanged(info, grad, near, far, edge)
    mine0 = summed_half(keep0, send0)
    other0 = swap_cores(mine0)
    extended, grad, near, far, edge, held = call(
        second_kernel, step_outs, info, extended, *moves,
        loads=loads, stores=(whole,), scratch=STEP_SCRATCH + HELD + SEMS,
    )
    moves = exchanged(info, grad, near, far, edge)
    own, grad, near, far, keep2, send2, probe = call(
        lambda *refs: third_kernel(rate, *refs), [HALF, HALF, STRIP, STRIP, HALF, HALF, whole],
        info, extended, *moves, mine0, other0,
        loads=loads + (held,), scratch=STEP_SCRATCH + HELD + SEMS,
    )
    cols = cols_swapped(near, far)
    near, far, center = call(
        last_middle_kernel, [EDGE, EDGE, HALF], info, grad, *cols, scratch=(PLACE,)
    )
    rows = rows_swapped(near, far)
    mine = summed_half(keep2, send2)
    other = swap_cores(mine)
    (obj,) = call(object_kernel, [HALF], info, own, center, *rows, on_chip=False)
    own_half = jnp.arange(2).reshape(2, 1, 1, 1) == core
    probe = probe.reshape(2, *HALF) - rate * jnp.where(own_half, mine, other)
    return obj.reshape(2, 2, WIN, WIN), probe.reshape(MODES, 2, WIN, WIN)


def solution(mesh):
    fine = Mesh(mesh.devices.reshape(SIZES), AXES)
    in_specs = (
        P(None, None, ROW, COL),
        P(),
        P(),
        P(None, ROW, COL, None, None),
        P(None, ROW, COL, None),
    )
    out_specs = (P(None, None, ROW, COL), P())
    return jax.shard_map(steps, mesh=fine, in_specs=in_specs, out_specs=out_specs, check_vma=False)
```
